256 devices in a mesh: ctx: 128 (over z, x, y_lo, core), head: 2 (over y_hi).
Axes of the slice: x: 4, y: 4 (y_hi: 2, y_lo: 2; y = y_hi * 2 + y_lo), z: 8, core: 2. Of those that a mesh axis runs over, the one named last changes fastest.
Arguments:
- queries: bfloat16 [16384, 2048], P('ctx', 'head'), may hold values from -12 to 12
- barred_key_rows: bfloat16 [16384, 512], P('ctx', 'head'), may hold values from -5.5 to 5.5
- barred_value_rows: bfloat16 [16384, 512], P('ctx', 'head'), may hold values from -12 to 12
- doc_start: int32 [16384], P('ctx'), may hold values from 0 to 16383, as said below
- out_weight: bfloat16 [2048, 4096], P('head'), may hold values from -0.5 to 0.5
Outputs:
- mixed: bfloat16 [16384, 4096], P('ctx', 'head')
The draws below stay inside these ranges and needn't reach their ends.
Inputs may be any that keep to these rules, and one draw needn't show every extreme that they name: Documents are runs of consecutive positions starting at position 0; the first has exactly 8192 tokens, each other has 2048 to 8192 tokens except the last two: the final position 16383 is a document of one token, and the one before it may be shorter; doc_start of a row is the first position of its document, so it is at most pos of that row.
All inputs are finite; a program needn't handle non-finite values.
Results may differ from the reference program's by a relative error of at most 0.015.
Values may be sent and summed in bfloat16 or wider, within the bound.
A program may use at most 128 MiB of HBM per device.

```python
import math
import jax
import jax.numpy as jnp
from jax import lax

D = 4096
QUERY_HEADS = 16
KEY_VALUE_HEADS = 4
HEAD_SIZE = 128
TOK_DEV = 128
STRIPE = 64
ROUNDS = 2
PACKED_TOKENS = 16384
DOCUMENT_LONGEST = 8192
DOC_MIN = 2048
N_CTX = 128


def barred_row_order(array):
    cycle_size = PACKED_TOKENS // TOK_DEV
    trailing = array.shape[1:]
    shaped = array.reshape((TOK_DEV // STRIPE, cycle_size, STRIPE) + trailing)
    return jnp.swapaxes(shaped, 0, 1).reshape((PACKED_TOKENS,) + trailing)


def paired(key):
    key_starting_row = jnp.clip(jax.random.normal(jax.random.fold_in(key, 11), (PACKED_TOKENS, KEY_VALUE_HEADS, HEAD_SIZE), jnp.float32), -5.5, 5.5)
    query_base = jnp.clip(3.0 * jax.random.normal(jax.random.fold_in(key, 12), (PACKED_TOKENS, QUERY_HEADS, HEAD_SIZE), jnp.float32), -12.0, 12.0)
    return (query_base, key_starting_row)


def draw_queries(key, part):
    query_base, key_starting_row = paired(key)
    return barred_row_order(query_base.reshape(PACKED_TOKENS, QUERY_HEADS * HEAD_SIZE)).astype(jnp.bfloat16)


def draw_barred_key_rows(key, part):
    query_base, key_starting_row = paired(key)
    return barred_row_order(key_starting_row.reshape(PACKED_TOKENS, KEY_VALUE_HEADS * HEAD_SIZE)).astype(jnp.bfloat16)


def draw_doc_start(key, part):
    doc_count = PACKED_TOKENS // DOC_MIN + 1
    lengths = jax.random.randint(jax.random.fold_in(key, 21), (doc_count,), DOC_MIN, DOCUMENT_LONGEST + 1)
    lengths = jnp.where(jnp.arange(doc_count) == 0, DOCUMENT_LONGEST, lengths).astype(jnp.int32)
    doc_ends = jnp.cumsum(lengths).astype(jnp.int32)
    starts = doc_ends - lengths
    row_index = jnp.arange(PACKED_TOKENS, dtype=jnp.int32)
    doc_index = jnp.sum((doc_ends[None, :] <= row_index[:, None]).astype(jnp.int32), axis=1)
    natural = starts[doc_index]
    natural = jnp.where(row_index == PACKED_TOKENS - 1, PACKED_TOKENS - 1, natural)
    return barred_row_order(natural).astype(jnp.int32)


def shard_levels(stream_key, dims, pieces, least, high):
    loudness = 1.0
    for axis_at, shards_of in pieces:
        steps = jax.random.uniform(jax.random.fold_in(jax.random.fold_in(stream_key, 6), axis_at), (shards_of,), jnp.float32, least / len(pieces), high / len(pieces))
        loudness = loudness * jnp.repeat(jnp.exp(steps), dims[axis_at] // shards_of).reshape((-1,) + (1,) * (len(dims) - 1 - axis_at))
    return loudness


def centred(key, extent, width, reach, pieces=(), kind=jnp.bfloat16):
    loudness = shard_levels(key, extent, pieces, -0.22, 0.18) if pieces else 1.0
    entries = jax.random.normal(key, extent, jnp.float32) * width * loudness
    return jnp.minimum(jnp.maximum(entries, -reach), reach).astype(kind)


def setup_inputs(seed: int = 0) -> dict:
    streams_of = jax.random.split(jax.random.key(seed), 6)
    queries = draw_queries(jax.random.fold_in(streams_of[5], 71), 0)
    barred_key_rows = draw_barred_key_rows(jax.random.fold_in(streams_of[5], 71), 0)
    barred_value_rows = centred(streams_of[2], (PACKED_TOKENS, KEY_VALUE_HEADS * HEAD_SIZE), 2.0, 12.0, ((0, 128), (1, 2)))
    doc_start = draw_doc_start(jax.random.fold_in(streams_of[5], 71), 0)
    out_weight = centred(streams_of[4], (QUERY_HEADS * HEAD_SIZE, D), HEAD_SIZE ** -0.5, 0.5, ((0, 2),))
    return {"queries": queries, "barred_key_rows": barred_key_rows, "barred_value_rows": barred_value_rows, "doc_start": doc_start, "out_weight": out_weight}


def restore_natural(array):
    trailing = array.shape[1:]
    shaped = array.reshape((N_CTX, ROUNDS, STRIPE) + trailing)
    return jnp.swapaxes(shaped, 0, 1).reshape((PACKED_TOKENS,) + trailing)

def restripe(array):
    trailing = array.shape[1:]
    shaped = array.reshape((ROUNDS, N_CTX, STRIPE) + trailing)
    return jnp.swapaxes(shaped, 0, 1).reshape((PACKED_TOKENS,) + trailing)

def reference(queries, barred_key_rows, barred_value_rows, doc_start, out_weight):
    heads_per_group = QUERY_HEADS // KEY_VALUE_HEADS
    query_natural_rows = restore_natural(queries).reshape(PACKED_TOKENS, KEY_VALUE_HEADS, heads_per_group, HEAD_SIZE)
    key_natural_rows = restore_natural(barred_key_rows).reshape(PACKED_TOKENS, KEY_VALUE_HEADS, HEAD_SIZE)
    value_natural_rows = restore_natural(barred_value_rows).reshape(PACKED_TOKENS, KEY_VALUE_HEADS, HEAD_SIZE)
    doc_nat = restore_natural(doc_start)
    block_rows = min(256, PACKED_TOKENS)
    pad_amount = jnp.zeros((DOCUMENT_LONGEST, KEY_VALUE_HEADS, HEAD_SIZE), jnp.bfloat16)
    key_pad = jnp.concatenate([pad_amount, key_natural_rows], axis=0)
    value_pad = jnp.concatenate([pad_amount, value_natural_rows], axis=0)
    window = DOCUMENT_LONGEST + block_rows
    score_scale = 1.0 / math.sqrt(HEAD_SIZE)

    def one_block(block_index):
        block_start = (block_index * block_rows).astype(jnp.int32)
        query_block = lax.dynamic_slice_in_dim(query_natural_rows, block_start, block_rows, 0).astype(jnp.float32)
        key_block = lax.dynamic_slice_in_dim(key_pad, block_start, window, 0).astype(jnp.float32)
        value_block = lax.dynamic_slice_in_dim(value_pad, block_start, window, 0).astype(jnp.float32)
        doc_block = lax.dynamic_slice_in_dim(doc_nat, block_start, block_rows, 0)
        query_pos = block_start + jnp.arange(block_rows, dtype=jnp.int32)
        key_pos = block_start - DOCUMENT_LONGEST + jnp.arange(window, dtype=jnp.int32)
        visible = (doc_block[:, None] <= key_pos[None, :]) & (key_pos[None, :] <= query_pos[:, None])
        scores = jnp.einsum('tkgd,nkd->kgtn', query_block, key_block) * score_scale
        scores = jnp.where(visible, scores, -1e+30)
        row_top = lax.optimization_barrier(jnp.max(scores, axis=-1, keepdims=True))
        weights = jnp.where(visible, jnp.exp(scores - row_top), 0.0).astype(jnp.bfloat16)
        weights_wide = weights.astype(jnp.float32)
        row_sum = lax.optimization_barrier(jnp.sum(weights_wide, axis=-1))
        summed = jnp.einsum('kgtn,nkd->tkgd', weights_wide, value_block)
        scaled = summed / jnp.transpose(row_sum, (2, 0, 1))[..., None]
        return scaled.reshape(block_rows, QUERY_HEADS * HEAD_SIZE).astype(jnp.bfloat16)
    blocks = lax.map(one_block, jnp.arange(PACKED_TOKENS // block_rows, dtype=jnp.int32))
    attn = restripe(blocks.reshape(PACKED_TOKENS, QUERY_HEADS * HEAD_SIZE))
    return jnp.dot(attn, out_weight, preferred_element_type=jnp.float32).astype(jnp.bfloat16)
```

```python
import math

import jax
import jax.numpy as jnp
from jax import lax
from jax.experimental import pallas as pl
from jax.experimental.pallas import tpu as pltpu
from jax.sharding import PartitionSpec as P

NZ, NX, NY, NC = 8, 4, 2, 2
STRIPE = 64
HEAD = 128
GROUP = 4
PLANE = NX * NY * NC * STRIPE
ROWS = GROUP * STRIPE
ROUND = NZ * PLANE
COLS = 2048
CHUNK = 256
NCH = COLS // CHUNK
MASKED = -1e30
LOG2 = math.log2(math.e) / math.sqrt(HEAD)
MESH = pl.DeviceIdType.MESH
F32 = jnp.float32
BF16 = jnp.bfloat16


def kernel(q_hbm, k_hbm, v_hbm, doc_hbm, w_hbm, out_ref,
           kv, q_in, doc_in, q_rows, doc_rows, top, acc, attn_send, attn_in, attn, w_own, part_send,
           relay, part_in, own_part,
           loc_sem, w_sem, kx_s, kx_r, qx_s, qx_r, dx_s, dx_r, z_s, z_r, c0_s, c0_r, c_s, c_r, y0_s, y0_r,
           y_s, y_r, o_s, o_r, p_s, p_r, f_s, f_r):
    c = lax.axis_index("ctx")
    h = lax.axis_index("head")
    z, x, y, core = c // 16, (c // 4) % NX, (c // 2) % NY, c % NC
    rnd = x // 2

    def dev(z_, x_, y_, k_, h_):
        return (((z_ * NX + x_) * NY + y_) * NC + k_, h_)

    up = dev((z + 1) % NZ, x, y, core, h)
    down = dev((z + NZ - 1) % NZ, x, y, core, h)
    across = dev(z, x, 1 - y, core, h)
    twin = dev(z, x, y, 1 - core, h)
    outer = dev(z, x, 1 - y, core, 1 - h)
    xs = [(x + d) % NX for d in (2, 1, 3)]

    def send(src, dst, ss, rs, to):
        cp = pltpu.make_async_remote_copy(src, dst, ss, rs, device_id=to, device_id_type=MESH)
        cp.start()

    def got(ref, ss, rs):
        pltpu.make_async_remote_copy(ref, ref, ss, rs, device_id=twin, device_id_type=MESH).wait_recv()

    def sent(ref, ss, rs):
        pltpu.make_async_remote_copy(ref, ref, ss, rs, device_id=twin, device_id_type=MESH).wait_send()

    barrier = pltpu.get_barrier_semaphore()
    peers = [up, down, across, twin, outer] + [dev(z, x_, y, core, h) for x_ in xs]
    for peer in peers:
        pl.semaphore_signal(barrier, inc=1, device_id=peer, device_id_type=MESH)

    def kv_src(ref, x_):
        return ref.at[pl.ds(pl.multiple_of(x_ // 2 * STRIPE, STRIPE), STRIPE),
                      pl.ds(pl.multiple_of(x_ % 2 * HEAD, HEAD), HEAD)]

    def q_src(x_):
        return q_hbm.at[pl.ds(pl.multiple_of(x_ // 2 * STRIPE, STRIPE), STRIPE),
                        pl.ds(pl.multiple_of(x_ % 2 * GROUP * HEAD, HEAD), GROUP * HEAD)]

    def doc_src(x_):
        return doc_hbm.at[pl.ds(pl.multiple_of(x_ // 2 * STRIPE, STRIPE), STRIPE)]

    own_copies = [
        pltpu.make_async_copy(kv_src(k_hbm, x), kv.at[z, x, y, core, 0], loc_sem.at[0]),
        pltpu.make_async_copy(kv_src(v_hbm, x), kv.at[z, x, y, core, 1], loc_sem.at[1]),
        pltpu.make_async_copy(q_src(x), q_in.at[x], loc_sem.at[2]),
        pltpu.make_async_copy(doc_src(x), doc_in.at[x], loc_sem.at[3]),
    ]
    for cp in own_copies:
        cp.start()
    pl.semaphore_wait(barrier, len(peers))

    for x_ in xs:
        to = dev(z, x_, y, core, h)
        send(kv_src(k_hbm, x_), kv.at[z, x, y, core, 0], kx_s.at[x_, 0], kx_r.at[x, 0], to)
        send(kv_src(v_hbm, x_), kv.at[z, x, y, core, 1], kx_s.at[x_, 1], kx_r.at[x, 1], to)
    for x_ in xs:
        to = dev(z, x_, y, core, h)
        send(q_src(x_), q_in.at[x], qx_s.at[x_], qx_r.at[x], to)
        send(doc_src(x_), doc_in.at[x], dx_s.at[x_], dx_r.at[x], to)

    w_copies = [
        pltpu.make_async_copy(w_hbm.at[:, pl.ds(pl.multiple_of((1 - h) * COLS, COLS), COLS)], w_own.at[0], w_sem.at[0]),
        pltpu.make_async_copy(w_hbm.at[:, pl.ds(pl.multiple_of(h * COLS, COLS), COLS)], w_own.at[1], w_sem.at[1]),
    ]

    def part_ref(zp, part, half=None):
        xb = 2 * (((part + 1) // 2 + 1) % 2)
        yy = (y + part // 2) % 2
        if half is None:
            return kv.at[zp, pl.ds(xb, 2), yy, core]
        return kv.at[zp, pl.ds(xb + half, 1), yy, core]

    own_copies[0].wait()
    own_copies[1].wait()
    for x_ in xs:
        got(kv.at[z, x_, y, core, 0], kx_s.at[x_, 0], kx_r.at[x_, 0])
        got(kv.at[z, x_, y, core, 1], kx_s.at[x_, 1], kx_r.at[x_, 1])
    for part in (1, 0):
        ref = part_ref(z, part)
        send(ref, ref, y0_s.at[part], y0_r.at[part], across)
        send(ref, ref, z_s.at[0, 0, part], z_r.at[0, 0, part], up)
        send(ref, ref, z_s.at[1, 0, part], z_r.at[1, 0, part], down)
        send(ref, ref, c0_s.at[part], c0_r.at[part], twin)
    for cp in w_copies:
        cp.start()
    ref = part_ref(z, 2)
    got(ref, y0_s.at[1], y0_r.at[1])
    send(ref, ref, z_s.at[0, 0, 2], z_r.at[0, 0, 2], up)
    send(ref, ref, z_s.at[1, 0, 2], z_r.at[1, 0, 2], down)
    send(ref, ref, c0_s.at[2], c0_r.at[2], twin)
    ref = part_ref(z, 3)
    got(ref, y0_s.at[0], y0_r.at[0])
    send(ref, ref, c0_s.at[3], c0_r.at[3], twin)

    def twin_ref(zp, part, half=None):
        xb = 2 * (((part + 1) // 2 + 1) % 2)
        yy = (y + part // 2) % 2
        if half is None:
            return kv.at[zp, pl.ds(xb, 2), yy, 1 - core]
        return kv.at[zp, pl.ds(xb + half, 1), yy, 1 - core]

    def work(plane, rb, own, docs):
        keys = kv[plane, :, :, :, 0].reshape(PLANE, HEAD)
        values = kv[plane, :, :, :, 1].reshape(PLANE, HEAD)
        s = lax.dot_general(q_rows[rb], keys, (((1,), (1,)), ((), ())), preferred_element_type=F32)
        if docs:
            kpos = rnd * ROUND + plane * PLANE + lax.broadcasted_iota(jnp.int32, (ROWS, PLANE), 1)
            seen = kpos >= jnp.tile(doc_rows[rb], (1, PLANE // HEAD))
            if own:
                first = rnd * ROUND + (z * 16 + rb * 4 + y * 2 + core) * STRIPE
                qpos = first + lax.broadcasted_iota(jnp.int32, (ROWS, PLANE), 0) % STRIPE
                seen = seen & (kpos <= qpos)
            s = jnp.where(seen, s, MASKED)
        old = top[rb]
        new = jnp.maximum(old, jnp.max(s, axis=1, keepdims=True))
        p = jnp.exp2(s * LOG2 - jnp.tile(new * LOG2, (1, PLANE // HEAD))).astype(BF16)
        shrink = jnp.exp2((old - new) * LOG2)
        both = jnp.concatenate([values, jnp.ones((PLANE, HEAD), BF16)], axis=1)
        acc[rb] = acc[rb] * jnp.tile(shrink, (1, 2)) + jnp.dot(p, both, preferred_element_type=F32)
        top[rb] = new

    def chunk(d, side, rb):
        plane = (z + NZ - d + 2 * d * side) % NZ
        earlier = (d > 0) & (plane < z)

        @pl.when((d == 0) & (side == 0))
        def _():
            work(z, rb, True, True)

        @pl.when(earlier & (rnd == 1))
        def _():
            work(plane, rb, False, True)

        @pl.when(earlier & (rnd == 0))
        def _():
            work(plane, rb, False, False)

    def event(t, carry):
        s = t // 8 + 1
        e = t % 8
        side, part = e % 2, e // 2
        plane = (z + NZ - s + 2 * s * side) % NZ
        nxt = dev((z + 1 + (NZ - 2) * side) % NZ, x, y, core, h)

        @pl.when((s <= 3) & (part <= 2))
        def _():
            got(part_ref(plane, part), z_s.at[side, s - 1, part], z_r.at[side, s - 1, part])

        @pl.when((s == 4) & (part <= 2))
        def _():
            got(part_ref(plane, part, side), z_s.at[side, 3, part], z_r.at[side, 3, part])

        @pl.when((s <= 3) & (part == 3))
        def _():
            got(part_ref(plane, 3), y_s.at[s - 1, side], y_r.at[s - 1, side])

        @pl.when((s == 4) & (part == 3))
        def _():
            got(part_ref(plane, 3, side), y_s.at[3, side], y_r.at[3, side])

        @pl.when((s <= 2) & (part <= 2))
        def _():
            r = part_ref(plane, part)
            send(r, r, z_s.at[side, s, part], z_r.at[side, s, part], nxt)

        @pl.when((s == 3) & (part <= 2))
        def _():
            r = part_ref(plane, part, side)
            send(r, r, z_s.at[side, 3, part], z_r.at[side, 3, part], nxt)

        @pl.when(s <= 3)
        def _():
            r = part_ref(plane, part)

            @pl.when(part == 0)
            def _():
                send(r, r, y_s.at[s - 1, side], y_r.at[s - 1, side], across)

            send(r, r, c_s.at[s - 1, side, part], c_r.at[s - 1, side, part], twin)

        @pl.when(s == 4)
        def _():
            r = part_ref(plane, part, side)

            @pl.when(part == 0)
            def _():
                send(r, r, y_s.at[3, side], y_r.at[3, side], across)

            send(r, r, c_s.at[3, side, part], c_r.at[3, side, part], twin)

        @pl.when(t == 0)
        def _():
            own_copies[2].wait()
            own_copies[3].wait()
            for x_ in xs:
                got(q_in.at[x_], qx_s.at[x_], qx_r.at[x_])
                got(doc_in.at[x_], dx_s.at[x_], dx_r.at[x_])
            for part_ in range(4):
                got(twin_ref(z, part_), c0_s.at[part_], c0_r.at[part_])
            for rb_ in range(NX):
                for g in range(GROUP):
                    q_rows[rb_, g * STRIPE:(g + 1) * STRIPE] = q_in[rb_, :, g * HEAD:(g + 1) * HEAD]
                    doc_rows[rb_, g * STRIPE:(g + 1) * STRIPE] = doc_in[rb_]
            top[...] = jnp.full(top.shape, MASKED, F32)
            acc[...] = jnp.zeros(acc.shape, F32)

        cs, rb = e // 4, e % 4

        @pl.when((s > 1) & (rb == 0))
        def _():
            back = (z + NZ - (s - 1) + 2 * (s - 1) * cs) % NZ
            for part_ in range(4):
                got(twin_ref(back, part_), c_s.at[s - 2, cs, part_], c_r.at[s - 2, cs, part_])

        chunk(s - 1, cs, rb)
        return carry

    lax.fori_loop(0, 32, event, 0)

    far = (z + 4) % NZ
    for side in range(2):
        for part in range(4):
            got(twin_ref(far, part, side), c_s.at[3, side, part], c_r.at[3, side, part])

    def last(rb, carry):
        chunk(4, 0, rb)
        total = acc[rb]
        o = (total[:, :HEAD] / total[:, HEAD:]).astype(BF16)
        for g in range(GROUP):
            attn_send[rb, :, g * HEAD:(g + 1) * HEAD] = o[g * STRIPE:(g + 1) * STRIPE]

        @pl.when(rb != x)
        def _():
            send(attn_send.at[rb], attn_in.at[x], o_s.at[rb], o_r.at[x], dev(z, rb, y, core, h))

        return carry

    lax.fori_loop(0, NX, last, 0)
    attn_in[x] = attn_send[x]

    for cp in w_copies:
        cp.wait()
    for x_ in xs:
        got(attn_in.at[x_], o_s.at[x_], o_r.at[x_])
    for kind in range(NX):
        attn[kind // 2 * STRIPE:(kind // 2 + 1) * STRIPE,
             kind % 2 * GROUP * HEAD:(kind % 2 + 1) * GROUP * HEAD] = attn_in[kind]

    for j in range(NCH):
        piece = jnp.dot(attn[...], w_own[0, :, j * CHUNK:(j + 1) * CHUNK], preferred_element_type=F32)
        part_send[j] = piece.astype(BF16)
        way, i = j % 2, j // 2
        send(part_send.at[j], relay.at[way, i], p_s.at[way, i], p_r.at[way, i], across if way == 0 else outer)
    for i in range(NCH // 2):
        for way in range(2):
            got(relay.at[way, i], p_s.at[way, i], p_r.at[way, i])
            send(relay.at[way, i], part_in.at[2 * i + way], f_s.at[way, i], f_r.at[way, i],
                 outer if way == 0 else across)
        for j in (2 * i, 2 * i + 1):
            own_part[:, j * CHUNK:(j + 1) * CHUNK] = jnp.dot(
                attn[...], w_own[1, :, j * CHUNK:(j + 1) * CHUNK], preferred_element_type=F32)
    for j in range(NCH):
        way, i = j % 2, j // 2
        got(part_in.at[j], f_s.at[way, i], f_r.at[way, i])
        cols = slice(j * CHUNK, (j + 1) * CHUNK)
        out_ref[:, cols] = (own_part[:, cols] + part_in[j].astype(F32)).astype(BF16)

    for x_ in xs:
        for n in range(2):
            sent(kv.at[z, x_, y, core, n], kx_s.at[x_, n], kx_r.at[x_, n])
        sent(q_in.at[x_], qx_s.at[x_], qx_r.at[x_])
        sent(doc_in.at[x_], dx_s.at[x_], dx_r.at[x_])
        sent(attn_send.at[x_], o_s.at[x_], o_r.at[x_])
    for part in range(2):
        sent(part_ref(z, part), y0_s.at[part], y0_r.at[part])
    for part in range(4):
        sent(part_ref(z, part), c0_s.at[part], c0_r.at[part])
    for n in range(4):
        for side in range(2):
            half = side if n == 3 else None
            for part in range(3):
                sent(part_ref(z, part, half), z_s.at[side, n, part], z_r.at[side, n, part])
            for part in range(4):
                sent(part_ref(z, part, half), c_s.at[n, side, part], c_r.at[n, side, part])
            sent(part_ref(z, 0, half), y_s.at[n, side], y_r.at[n, side])
    for way in range(2):
        for i in range(NCH // 2):
            sent(relay.at[way, i], p_s.at[way, i], p_r.at[way, i])
            sent(relay.at[way, i], f_s.at[way, i], f_r.at[way, i])


def local(queries, keys, values, doc_start, out_weight):
    docs = jnp.broadcast_to(doc_start[:, None], (doc_start.shape[0], HEAD))
    dma = pltpu.SemaphoreType.DMA
    anyspace = pl.BlockSpec(memory_space=pl.ANY)
    return pl.pallas_call(
        kernel,
        out_shape=jax.ShapeDtypeStruct((2 * STRIPE, COLS), BF16),
        in_specs=[anyspace] * 5,
        out_specs=pl.BlockSpec(memory_space=pltpu.VMEM),
        scratch_shapes=[
            pltpu.VMEM((NZ, NX, NY, NC, 2, STRIPE, HEAD), BF16),
            pltpu.VMEM((NX, STRIPE, GROUP * HEAD), BF16),
            pltpu.VMEM((NX, STRIPE, HEAD), jnp.int32),
            pltpu.VMEM((NX, ROWS, HEAD), BF16),
            pltpu.VMEM((NX, ROWS, HEAD), jnp.int32),
            pltpu.VMEM((NX, ROWS, HEAD), F32),
            pltpu.VMEM((NX, ROWS, 2 * HEAD), F32),
            pltpu.VMEM((NX, STRIPE, GROUP * HEAD), BF16),
            pltpu.VMEM((NX, STRIPE, GROUP * HEAD), BF16),
            pltpu.VMEM((2 * STRIPE, 2 * GROUP * HEAD), BF16),
            pltpu.VMEM((2, 2 * GROUP * HEAD, COLS), BF16),
            pltpu.VMEM((NCH, 2 * STRIPE, CHUNK), BF16),
            pltpu.VMEM((2, NCH // 2, 2 * STRIPE, CHUNK), BF16),
            pltpu.VMEM((NCH, 2 * STRIPE, CHUNK), BF16),
            pltpu.VMEM((2 * STRIPE, COLS), F32),
            dma((4,)), dma((2,)),
            dma((NX, 2)), dma((NX, 2)), dma((NX,)), dma((NX,)), dma((NX,)), dma((NX,)),
            dma((2, 4, 3)), dma((2, 4, 3)), dma((4,)), dma((4,)), dma((4, 2, 4)), dma((4, 2, 4)),
            dma((2,)), dma((2,)), dma((4, 2)), dma((4, 2)), dma((NX,)), dma((NX,)),
            dma((2, NCH // 2)), dma((2, NCH // 2)), dma((2, NCH // 2)), dma((2, NCH // 2)),
        ],
        compiler_params=pltpu.CompilerParams(
            collective_id=0, has_side_effects=True, vmem_limit_bytes=56 * 1024 * 1024),
    )(queries, keys, values, docs, out_weight)


def solution(mesh):
    placed = (P("ctx", "head"), P("ctx", "head"), P("ctx", "head"), P("ctx"), P("head", None))
    return jax.shard_map(local, mesh=mesh, in_specs=placed, out_specs=P("ctx", "head"), check_vma=False)
```

```python
import math

import jax
import jax.numpy as jnp
from jax import lax
from jax.experimental import pallas as pl
from jax.experimental.pallas import tpu as pltpu
from jax.sharding import PartitionSpec as P

NZ, NX, NY, NC = 8, 4, 2, 2
STRIPE = 64
HEAD = 128
GROUP = 4
PLANE = NX * NY * NC * STRIPE
ROWS = GROUP * STRIPE
BLOCK = NY * NC * STRIPE
ROUND = NZ * PLANE
COLS = 2048
CHUNK = 256
NCH = COLS // CHUNK
MASKED = -1e30
LOG2 = math.log2(math.e) / math.sqrt(HEAD)
MESH = pl.DeviceIdType.MESH
F32 = jnp.float32
BF16 = jnp.bfloat16


def kernel(q_hbm, k_hbm, v_hbm, doc_hbm, w_hbm, out_ref,
           kv, q_in, doc_in, q_rows, doc_rows, top, acc, attn_send, attn_in, attn, w_own, part_send,
           part_in, own_part,
           loc_sem, w_sem, kx_s, kx_r, qx_s, qx_r, dx_s, dx_r, z_s, z_r, c0_s, c0_r, c_s, c_r, y0_s, y0_r,
           y_s, y_r, o_s, o_r, p_s, p_r):
    c = lax.axis_index("ctx")
    h = lax.axis_index("head")
    z, x, y, core = c // 16, (c // 4) % NX, (c // 2) % NY, c % NC
    rnd = x // 2

    def dev(z_, x_, y_, k_, h_):
        return (((z_ * NX + x_) * NY + y_) * NC + k_, h_)

    up = dev((z + 1) % NZ, x, y, core, h)
    down = dev((z + NZ - 1) % NZ, x, y, core, h)
    across = dev(z, x, 1 - y, core, h)
    twin = dev(z, x, y, 1 - core, h)
    partner = dev(z, x, y, core, 1 - h)
    xs = [(x + d) % NX for d in (2, 1, 3)]

    def send(src, dst, ss, rs, to):
        cp = pltpu.make_async_remote_copy(src, dst, ss, rs, device_id=to, device_id_type=MESH)
        cp.start()

    def got(ref, ss, rs):
        pltpu.make_async_remote_copy(ref, ref, ss, rs, device_id=twin, device_id_type=MESH).wait_recv()

    def sent(ref, ss, rs):
        pltpu.make_async_remote_copy(ref, ref, ss, rs, device_id=twin, device_id_type=MESH).wait_send()

    barrier = pltpu.get_barrier_semaphore()
    peers = [up, down, across, twin, partner] + [dev(z, x_, y, core, h) for x_ in xs]
    for peer in peers:
        pl.semaphore_signal(barrier, inc=1, device_id=peer, device_id_type=MESH)

    def kv_src(ref, x_):
        return ref.at[pl.ds(pl.multiple_of(x_ // 2 * STRIPE, STRIPE), STRIPE),
                      pl.ds(pl.multiple_of(x_ % 2 * HEAD, HEAD), HEAD)]

    def q_src(x_):
        return q_hbm.at[pl.ds(pl.multiple_of(x_ // 2 * STRIPE, STRIPE), STRIPE),
                        pl.ds(pl.multiple_of(x_ % 2 * GROUP * HEAD, HEAD), GROUP * HEAD)]

    own_copies = [
        pltpu.make_async_copy(kv_src(k_hbm, x), kv.at[z, x, y, core, 0], loc_sem.at[0]),
        pltpu.make_async_copy(kv_src(v_hbm, x), kv.at[z, x, y, core, 1], loc_sem.at[1]),
        pltpu.make_async_copy(q_src(x), q_in.at[x], loc_sem.at[2]),
        pltpu.make_async_copy(doc_hbm, doc_in.at[x], loc_sem.at[3]),
    ]
    for cp in own_copies:
        cp.start()
    pl.semaphore_wait(barrier, len(peers))

    for x_ in xs:
        to = dev(z, x_, y, core, h)
        send(kv_src(k_hbm, x_), kv.at[z, x, y, core, 0], kx_s.at[x_, 0], kx_r.at[x, 0], to)
        send(kv_src(v_hbm, x_), kv.at[z, x, y, core, 1], kx_s.at[x_, 1], kx_r.at[x, 1], to)
    for x_ in xs:
        to = dev(z, x_, y, core, h)
        send(q_src(x_), q_in.at[x], qx_s.at[x_], qx_r.at[x], to)
        send(doc_hbm, doc_in.at[x], dx_s.at[x_], dx_r.at[x], to)

    w_copies = [
        pltpu.make_async_copy(w_hbm.at[:, pl.ds(pl.multiple_of((1 - h) * COLS, COLS), COLS)], w_own.at[0], w_sem.at[0]),
        pltpu.make_async_copy(w_hbm.at[:, pl.ds(pl.multiple_of(h * COLS, COLS), COLS)], w_own.at[1], w_sem.at[1]),
    ]

    def part_ref(zp, part, half=None):
        xb = 2 * (((part + 1) // 2 + 1) % 2)
        yy = (y + part // 2) % 2
        if half is None:
            return kv.at[zp, pl.ds(xb, 2), yy, core]
        return kv.at[zp, pl.ds(xb + half, 1), yy, core]

    own_copies[0].wait()
    own_copies[1].wait()
    for x_ in xs:
        got(kv.at[z, x_, y, core, 0], kx_s.at[x_, 0], kx_r.at[x_, 0])
        got(kv.at[z, x_, y, core, 1], kx_s.at[x_, 1], kx_r.at[x_, 1])
    for part in (1, 0):
        ref = part_ref(z, part)
        send(ref, ref, y0_s.at[part], y0_r.at[part], across)
        send(ref, ref, z_s.at[0, 0, part], z_r.at[0, 0, part], up)
        send(ref, ref, z_s.at[1, 0, part], z_r.at[1, 0, part], down)
        send(ref, ref, c0_s.at[part], c0_r.at[part], twin)
    for cp in w_copies:
        cp.start()
    ref = part_ref(z, 2)
    got(ref, y0_s.at[1], y0_r.at[1])
    send(ref, ref, z_s.at[0, 0, 2], z_r.at[0, 0, 2], up)
    send(ref, ref, z_s.at[1, 0, 2], z_r.at[1, 0, 2], down)
    send(ref, ref, c0_s.at[2], c0_r.at[2], twin)
    ref = part_ref(z, 3)
    got(ref, y0_s.at[0], y0_r.at[0])
    send(ref, ref, c0_s.at[3], c0_r.at[3], twin)

    def twin_ref(zp, part, half=None):
        xb = 2 * (((part + 1) // 2 + 1) % 2)
        yy = (y + part // 2) % 2
        if half is None:
            return kv.at[zp, pl.ds(xb, 2), yy, 1 - core]
        return kv.at[zp, pl.ds(xb + half, 1), yy, 1 - core]

    def work(plane, rb, own, docs):
        def scores(b):
            keys = kv[plane, b, :, :, 0].reshape(BLOCK, HEAD)
            s = lax.dot_general(q_rows[rb], keys, (((1,), (1,)), ((), ())), preferred_element_type=F32)
            if docs:
                kpos = rnd * ROUND + plane * PLANE + b * BLOCK + lax.broadcasted_iota(jnp.int32, (ROWS, BLOCK), 1)
                seen = kpos >= jnp.tile(doc_rows[rb], (1, BLOCK // HEAD))
                if own:
                    first = rnd * ROUND + (z * 16 + rb * 4 + y * 2 + core) * STRIPE
                    qpos = first + lax.broadcasted_iota(jnp.int32, (ROWS, BLOCK), 0) % STRIPE
                    seen = seen & (kpos <= qpos)
                s = jnp.where(seen, s, MASKED)
            return s

        old, total = top[rb], acc[rb]
        s = scores(0)
        for b in range(NX):
            ahead = scores(b + 1) if b + 1 < NX else None
            new = jnp.maximum(old, jnp.max(s, axis=1, keepdims=True))
            p = jnp.exp2(s * LOG2 - jnp.tile(new * LOG2, (1, BLOCK // HEAD))).astype(BF16)
            shrink = jnp.exp2((old - new) * LOG2)
            values = kv[plane, b, :, :, 1].reshape(BLOCK, HEAD)
            both = jnp.concatenate([values, jnp.ones((BLOCK, HEAD), BF16)], axis=1)
            total = total * jnp.tile(shrink, (1, 2)) + jnp.dot(p, both, preferred_element_type=F32)
            old, s = new, ahead
        acc[rb] = total
        top[rb] = old

    def chunk(d, side, rb):
        plane = (z + NZ - d + 2 * d * side) % NZ
        earlier = (d > 0) & (plane < z)

        @pl.when((d == 0) & (side == 0))
        def _():
            work(z, rb, True, True)

        @pl.when(earlier & (rnd == 1))
        def _():
            work(plane, rb, False, True)

        @pl.when(earlier & (rnd == 0))
        def _():
            work(plane, rb, False, False)

    def event(t, carry):
        s = t // 8 + 1
        e = t % 8
        side, part = e % 2, e // 2
        plane = (z + NZ - s + 2 * s * side) % NZ
        nxt = dev((z + 1 + (NZ - 2) * side) % NZ, x, y, core, h)

        @pl.when((s <= 3) & (part <= 2))
        def _():
            got(part_ref(plane, part), z_s.at[side, s - 1, part], z_r.at[side, s - 1, part])

        @pl.when((s == 4) & (part <= 2))
        def _():
            got(part_ref(plane, part, side), z_s.at[side, 3, part], z_r.at[side, 3, part])

        @pl.when((s <= 3) & (part == 3))
        def _():
            got(part_ref(plane, 3), y_s.at[s - 1, side], y_r.at[s - 1, side])

        @pl.when((s == 4) & (part == 3))
        def _():
            got(part_ref(plane, 3, side), y_s.at[3, side], y_r.at[3, side])

        @pl.when((s <= 2) & (part <= 2))
        def _():
            r = part_ref(plane, part)
            send(r, r, z_s.at[side, s, part], z_r.at[side, s, part], nxt)

        @pl.when((s == 3) & (part <= 2))
        def _():
            r = part_ref(plane, part, side)
            send(r, r, z_s.at[side, 3, part], z_r.at[side, 3, part], nxt)

        @pl.when(s <= 3)
        def _():
            r = part_ref(plane, part)

            @pl.when(part == 0)
            def _():
                send(r, r, y_s.at[s - 1, side], y_r.at[s - 1, side], across)

            send(r, r, c_s.at[s - 1, side, part], c_r.at[s - 1, side, part], twin)

        @pl.when(s == 4)
        def _():
            r = part_ref(plane, part, side)

            @pl.when(part == 0)
            def _():
                send(r, r, y_s.at[3, side], y_r.at[3, side], across)

            send(r, r, c_s.at[3, side, part], c_r.at[3, side, part], twin)

        @pl.when(t == 0)
        def _():
            own_copies[2].wait()
            own_copies[3].wait()
            for x_ in xs:
                got(q_in.at[x_], qx_s.at[x_], qx_r.at[x_])
                got(doc_in.at[x_], dx_s.at[x_], dx_r.at[x_])
            for part_ in range(4):
                got(twin_ref(z, part_), c0_s.at[part_], c0_r.at[part_])
            for rb_ in range(NX):
                line = jnp.broadcast_to(doc_in[rb_].astype(F32), (HEAD, HEAD))
                line = jnp.transpose(line).astype(jnp.int32)
                line = jnp.where(rnd == 1, line[STRIPE:], line[:STRIPE])
                for g in range(GROUP):
                    q_rows[rb_, g * STRIPE:(g + 1) * STRIPE] = q_in[rb_, :, g * HEAD:(g + 1) * HEAD]
                    doc_rows[rb_, g * STRIPE:(g + 1) * STRIPE] = line
            top[...] = jnp.full(top.shape, MASKED, F32)
            acc[...] = jnp.zeros(acc.shape, F32)

        cs, rb = e // 4, e % 4

        @pl.when((s > 1) & (rb == 0))
        def _():
            back = (z + NZ - (s - 1) + 2 * (s - 1) * cs) % NZ
            for part_ in range(4):
                got(twin_ref(back, part_), c_s.at[s - 2, cs, part_], c_r.at[s - 2, cs, part_])

        chunk(s - 1, cs, rb)
        return carry

    lax.fori_loop(0, 32, event, 0)

    far = (z + 4) % NZ
    for side in range(2):
        for part in range(4):
            got(twin_ref(far, part, side), c_s.at[3, side, part], c_r.at[3, side, part])

    def last(rb, carry):
        chunk(4, 0, rb)
        total = acc[rb]
        o = (total[:, :HEAD] / total[:, HEAD:]).astype(BF16)
        for g in range(GROUP):
            attn_send[rb, :, g * HEAD:(g + 1) * HEAD] = o[g * STRIPE:(g + 1) * STRIPE]

        @pl.when(rb != x)
        def _():
            send(attn_send.at[rb], attn_in.at[x], o_s.at[rb], o_r.at[x], dev(z, rb, y, core, h))

        return carry

    lax.fori_loop(0, NX, last, 0)
    attn_in[x] = attn_send[x]

    for cp in w_copies:
        cp.wait()
    for x_ in xs:
        got(attn_in.at[x_], o_s.at[x_], o_r.at[x_])
    for kind in range(NX):
        attn[kind // 2 * STRIPE:(kind // 2 + 1) * STRIPE,
             kind % 2 * GROUP * HEAD:(kind % 2 + 1) * GROUP * HEAD] = attn_in[kind]

    def theirs(j, carry):
        cols = pl.ds(pl.multiple_of(j * CHUNK, CHUNK), CHUNK)
        part_send[j] = jnp.dot(attn[...], w_own[0, :, cols], preferred_element_type=F32).astype(BF16)
        send(part_send.at[j], part_in.at[j], p_s.at[j], p_r.at[j], partner)
        return carry

    def ours(j, carry):
        cols = pl.ds(pl.multiple_of(j * CHUNK, CHUNK), CHUNK)
        own_part[:, cols] = jnp.dot(attn[...], w_own[1, :, cols], preferred_element_type=F32)
        return carry

    def joined(j, carry):
        got(part_in.at[j], p_s.at[j], p_r.at[j])
        cols = pl.ds(pl.multiple_of(j * CHUNK, CHUNK), CHUNK)
        out_ref[:, cols] = (own_part[:, cols] + part_in[j].astype(F32)).astype(BF16)
        return carry

    lax.fori_loop(0, NCH, theirs, 0)
    lax.fori_loop(0, NCH, ours, 0)
    lax.fori_loop(0, NCH, joined, 0)

    for x_ in xs:
        for n in range(2):
            sent(kv.at[z, x_, y, core, n], kx_s.at[x_, n], kx_r.at[x_, n])
        sent(q_in.at[x_], qx_s.at[x_], qx_r.at[x_])
        sent(doc_in.at[x_], dx_s.at[x_], dx_r.at[x_])
        sent(attn_send.at[x_], o_s.at[x_], o_r.at[x_])
    for part in range(2):
        sent(part_ref(z, part), y0_s.at[part], y0_r.at[part])
    for part in range(4):
        sent(part_ref(z, part), c0_s.at[part], c0_r.at[part])
    for n in range(4):
        for side in range(2):
            half = side if n == 3 else None
            for part in range(3):
                sent(part_ref(z, part, half), z_s.at[side, n, part], z_r.at[side, n, part])
            for part in range(4):
                sent(part_ref(z, part, half), c_s.at[n, side, part], c_r.at[n, side, part])
            sent(part_ref(z, 0, half), y_s.at[n, side], y_r.at[n, side])
    for j in range(NCH):
        sent(part_send.at[j], p_s.at[j], p_r.at[j])


def local(queries, keys, values, doc_start, out_weight):
    docs = doc_start.reshape(1, doc_start.shape[0])
    dma = pltpu.SemaphoreType.DMA
    anyspace = pl.BlockSpec(memory_space=pl.ANY)
    return pl.pallas_call(
        kernel,
        out_shape=jax.ShapeDtypeStruct((2 * STRIPE, COLS), BF16),
        in_specs=[anyspace] * 5,
        out_specs=pl.BlockSpec(memory_space=pltpu.VMEM),
        scratch_shapes=[
            pltpu.VMEM((NZ, NX, NY, NC, 2, STRIPE, HEAD), BF16),
            pltpu.VMEM((NX, STRIPE, GROUP * HEAD), BF16),
            pltpu.VMEM((NX, 1, HEAD), jnp.int32),
            pltpu.VMEM((NX, ROWS, HEAD), BF16),
            pltpu.VMEM((NX, ROWS, HEAD), jnp.int32),
            pltpu.VMEM((NX, ROWS, HEAD), F32),
            pltpu.VMEM((NX, ROWS, 2 * HEAD), F32),
            pltpu.VMEM((NX, STRIPE, GROUP * HEAD), BF16),
            pltpu.VMEM((NX, STRIPE, GROUP * HEAD), BF16),
            pltpu.VMEM((2 * STRIPE, 2 * GROUP * HEAD), BF16),
            pltpu.VMEM((2, 2 * GROUP * HEAD, COLS), BF16),
            pltpu.VMEM((NCH, 2 * STRIPE, CHUNK), BF16),
            pltpu.VMEM((NCH, 2 * STRIPE, CHUNK), BF16),
            pltpu.VMEM((2 * STRIPE, COLS), F32),
            dma((4,)), dma((2,)),
            dma((NX, 2)), dma((NX, 2)), dma((NX,)), dma((NX,)), dma((NX,)), dma((NX,)),
            dma((2, 4, 3)), dma((2, 4, 3)), dma((4,)), dma((4,)), dma((4, 2, 4)), dma((4, 2, 4)),
            dma((2,)), dma((2,)), dma((4, 2)), dma((4, 2)), dma((NX,)), dma((NX,)),
            dma((NCH,)), dma((NCH,)),
        ],
        compiler_params=pltpu.CompilerParams(
            collective_id=0, has_side_effects=True, vmem_limit_bytes=56 * 1024 * 1024),
    )(queries, keys, values, docs, out_weight)


def solution(mesh):
    placed = (P("ctx", "head"), P("ctx", "head"), P("ctx", "head"), P("ctx"), P("head", None))
    return jax.shard_map(local, mesh=mesh, in_specs=placed, out_specs=P("ctx", "head"), check_vma=False)
```

```python
import math

import jax
import jax.numpy as jnp
from jax import lax
from jax.experimental import pallas as pl
from jax.experimental.pallas import tpu as pltpu
from jax.sharding import PartitionSpec as P

NZ, NX, NY, NC = 8, 4, 2, 2
STRIPE = 64
HEAD = 128
GROUP = 4
PLANE = NX * NY * NC * STRIPE
ROWS = GROUP * STRIPE
BLOCK = NY * NC * STRIPE
ROUND = NZ * PLANE
COLS = 2048
CHUNK = 256
NCH = COLS // CHUNK
NPIECE = 4
WROWS = 2 * GROUP * HEAD // (NX * NC * NPIECE)
WLAG = 18
MASKED = -1e30
LOG2 = math.log2(math.e) / math.sqrt(HEAD)
MESH = pl.DeviceIdType.MESH
F32 = jnp.float32
BF16 = jnp.bfloat16


def kernel(q_hbm, k_hbm, v_hbm, doc_hbm, w_hbm, out_ref,
           kv, q_in, doc_in, q_rows, doc_rows, top, acc, attn_send, attn_in, attn_far, w_own, w_far,
           own_part,
           loc_sem, w_sem, kx_s, kx_r, qx_s, qx_r, dx_s, dx_r, z_s, z_r, c0_s, c0_r, c_s, c_r,
           y_s, y_r, o_s, o_r, of_s, of_r, wo_s, wo_r, wx_s, wx_r, wy_s, wy_r, wt_s, wt_r):
    c = lax.axis_index("ctx")
    h = lax.axis_index("head")
    z, x, y, core = c // 16, (c // 4) % NX, (c // 2) % NY, c % NC
    rnd = x // 2

    def dev(z_, x_, y_, k_, h_):
        return (((z_ * NX + x_) * NY + y_) * NC + k_, h_)

    up = dev((z + 1) % NZ, x, y, core, h)
    down = dev((z + NZ - 1) % NZ, x, y, core, h)
    across = dev(z, x, 1 - y, core, h)
    twin = dev(z, x, y, 1 - core, h)
    outer = dev(z, x, 1 - y, core, 1 - h)
    right, left = (x + 1) % NX, (x + NX - 1) % NX
    xs = [(x + d) % NX for d in (2, 1, 3)]

    def send(src, dst, ss, rs, to):
        cp = pltpu.make_async_remote_copy(src, dst, ss, rs, device_id=to, device_id_type=MESH)
        cp.start()

    def got(ref, ss, rs):
        pltpu.make_async_remote_copy(ref, ref, ss, rs, device_id=twin, device_id_type=MESH).wait_recv()

    def sent(ref, ss, rs):
        pltpu.make_async_remote_copy(ref, ref, ss, rs, device_id=twin, device_id_type=MESH).wait_send()

    barrier = pltpu.get_barrier_semaphore()
    peers = [up, down, across, twin, outer] + [dev(z, x_, y, core, h) for x_ in xs]
    peers += [dev(z, x_, 1 - y, core, h) for x_ in xs]
    peers += [dev(z, x_, y, core, 1 - h) for x_ in range(NX)]
    for peer in peers:
        pl.semaphore_signal(barrier, inc=1, device_id=peer, device_id_type=MESH)

    def kv_src(ref, x_):
        return ref.at[pl.ds(pl.multiple_of(x_ // 2 * STRIPE, STRIPE), STRIPE),
                      pl.ds(pl.multiple_of(x_ % 2 * HEAD, HEAD), HEAD)]

    def q_src(x_):
        return q_hbm.at[pl.ds(pl.multiple_of(x_ // 2 * STRIPE, STRIPE), STRIPE),
                        pl.ds(pl.multiple_of(x_ % 2 * GROUP * HEAD, HEAD), GROUP * HEAD)]

    own_copies = [
        pltpu.make_async_copy(kv_src(k_hbm, x), kv.at[z, x, y, core, 0], loc_sem.at[0]),
        pltpu.make_async_copy(kv_src(v_hbm, x), kv.at[z, x, y, core, 1], loc_sem.at[1]),
        pltpu.make_async_copy(q_src(x), q_in.at[x], loc_sem.at[2]),
        pltpu.make_async_copy(doc_hbm, doc_in.at[x], loc_sem.at[3]),
    ]
    for cp in own_copies:
        cp.start()
    pl.semaphore_wait(barrier, len(peers))

    for y_, d_ in ((y, 0), (1 - y, 1)):
        for x_ in (xs if d_ == 0 else xs + [x]):
            for n, ref in enumerate((k_hbm, v_hbm)):
                send(kv_src(ref, x_), kv.at[z, x, y, core, n], kx_s.at[d_, x_, n], kx_r.at[d_, x, n],
                     dev(z, x_, y_, core, h))
    for x_ in xs:
        to = dev(z, x_, y, core, h)
        send(q_src(x_), q_in.at[x], qx_s.at[x_], qx_r.at[x], to)
        send(doc_hbm, doc_in.at[x], dx_s.at[x_], dx_r.at[x], to)

    def w_rows(x_, k_, i_):
        return pl.ds(pl.multiple_of((x_ * NC + k_) * NPIECE * WROWS + i_ * WROWS, WROWS), WROWS)

    def w_piece(x_, k_, i_):
        return w_far.at[w_rows(x_, k_, i_)]

    for i in range(NPIECE):
        send(w_hbm.at[w_rows(x, core, i), pl.ds(pl.multiple_of((1 - h) * COLS, COLS), COLS)],
             w_piece(x, core, i), wo_s.at[i], wo_r.at[i], outer)

    def w_first(i):
        ref = w_piece(x, core, i)
        got(ref, wo_s.at[i], wo_r.at[i])
        send(ref, ref, wx_s.at[0, i], wx_r.at[0, i], dev(z, right, y, core, h))
        send(ref, ref, wx_s.at[1, i], wx_r.at[1, i], dev(z, left, y, core, h))
        send(ref, ref, wt_s.at[0, i], wt_r.at[0, i], twin)

    def w_second(i):
        for side, (src, dst) in enumerate(((left, right), (right, left))):
            ref = w_piece(src, core, i)
            got(ref, wx_s.at[side, i], wx_r.at[side, i])

            @pl.when(i // (NPIECE // 2) == side)
            def _():
                n = i % (NPIECE // 2)
                send(ref, ref, wy_s.at[side, n], wy_r.at[side, n], dev(z, dst, y, core, h))

            send(ref, ref, wt_s.at[1 + side, i], wt_r.at[1 + side, i], twin)

    def w_third(n):
        for side in range(2):
            i = side * (NPIECE // 2) + n
            ref = w_piece((x + 2) % NX, core, i)
            got(ref, wy_s.at[side, n], wy_r.at[side, n])
            send(ref, ref, wt_s.at[3, i], wt_r.at[3, i], twin)

    w_copy = pltpu.make_async_copy(w_hbm.at[:, pl.ds(pl.multiple_of(h * COLS, COLS), COLS)], w_own, w_sem.at[0])

    def part_ref(zp, part, half=None):
        xb = 2 * (((part + 1) // 2 + 1) % 2)
        yy = (y + part // 2) % 2
        if half is None:
            return kv.at[zp, pl.ds(xb, 2), yy, core]
        return kv.at[zp, pl.ds(xb + half, 1), yy, core]

    def own_part_in(part):
        d_ = part // 2
        for half in range(2):
            x_ = 2 * (((part + 1) // 2 + 1) % 2) + half

            def arrive():
                for n in range(2):
                    got(kv.at[z, x_, (y + d_) % 2, core, n], kx_s.at[d_, x_, n], kx_r.at[d_, x_, n])

            if d_:
                arrive()
            else:
                pl.when(x_ != x)(arrive)

    own_copies[0].wait()
    own_copies[1].wait()
    for part in (0, 1, 2, 3):
        own_part_in(part)
        ref = part_ref(z, part)
        if part < 3:
            send(ref, ref, z_s.at[0, 0, part], z_r.at[0, 0, part], up)
            send(ref, ref, z_s.at[1, 0, part], z_r.at[1, 0, part], down)
        send(ref, ref, c0_s.at[part], c0_r.at[part], twin)
    w_copy.start()

    def twin_ref(zp, part, half=None):
        xb = 2 * (((part + 1) // 2 + 1) % 2)
        yy = (y + part // 2) % 2
        if half is None:
            return kv.at[zp, pl.ds(xb, 2), yy, 1 - core]
        return kv.at[zp, pl.ds(xb + half, 1), yy, 1 - core]

    def work(plane, rb, own, docs):
        def scores(b):
            keys = kv[plane, b, :, :, 0].reshape(BLOCK, HEAD)
            s = lax.dot_general(q_rows[rb], keys, (((1,), (1,)), ((), ())), preferred_element_type=F32)
            if docs:
                kpos = rnd * ROUND + plane * PLANE + b * BLOCK + lax.broadcasted_iota(jnp.int32, (ROWS, BLOCK), 1)
                seen = kpos >= jnp.tile(doc_rows[rb], (1, BLOCK // HEAD))
                if own:
                    first = rnd * ROUND + (z * 16 + rb * 4 + y * 2 + core) * STRIPE
                    qpos = first + lax.broadcasted_iota(jnp.int32, (ROWS, BLOCK), 0) % STRIPE
                    seen = seen & (kpos <= qpos)
                s = jnp.where(seen, s, MASKED)
            return s

        old, total = top[rb], acc[rb]
        s = scores(0)
        for b in range(NX):
            ahead = scores(b + 1) if b + 1 < NX else None
            new = jnp.maximum(old, jnp.max(s, axis=1, keepdims=True))
            p = jnp.exp2(s * LOG2 - jnp.tile(new * LOG2, (1, BLOCK // HEAD))).astype(BF16)
            shrink = jnp.exp2((old - new) * LOG2)
            values = kv[plane, b, :, :, 1].reshape(BLOCK, HEAD)
            both = jnp.concatenate([values, jnp.ones((BLOCK, HEAD), BF16)], axis=1)
            total = total * jnp.tile(shrink, (1, 2)) + jnp.dot(p, both, preferred_element_type=F32)
            old, s = new, ahead
        acc[rb] = total
        top[rb] = old

    def chunk(d, side, rb):
        plane = (z + NZ - d + 2 * d * side) % NZ
        earlier = (d > 0) & (plane < z)

        @pl.when((d == 0) & (side == 0))
        def _():
            work(z, rb, True, True)

        @pl.when(earlier & (rnd == 1))
        def _():
            work(plane, rb, False, True)

        @pl.when(earlier & (rnd == 0))
        def _():
            work(plane, rb, False, False)

    def event(t, carry):
        s = t // 8 + 1
        e = t % 8
        side, part = e % 2, e // 2
        plane = (z + NZ - s + 2 * s * side) % NZ
        nxt = dev((z + 1 + (NZ - 2) * side) % NZ, x, y, core, h)

        @pl.when((s <= 3) & (part <= 2))
        def _():
            got(part_ref(plane, part), z_s.at[side, s - 1, part], z_r.at[side, s - 1, part])

        @pl.when((s == 4) & (part <= 2))
        def _():
            got(part_ref(plane, part, side), z_s.at[side, 3, part], z_r.at[side, 3, part])

        @pl.when((s <= 3) & (part == 3))
        def _():
            got(part_ref(plane, 3), y_s.at[s - 1, side], y_r.at[s - 1, side])

        @pl.when((s == 4) & (part == 3))
        def _():
            got(part_ref(plane, 3, side), y_s.at[3, side], y_r.at[3, side])

        @pl.when((s <= 2) & (part <= 2))
        def _():
            r = part_ref(plane, part)
            send(r, r, z_s.at[side, s, part], z_r.at[side, s, part], nxt)

        @pl.when((s == 3) & (part <= 2))
        def _():
            r = part_ref(plane, part, side)
            send(r, r, z_s.at[side, 3, part], z_r.at[side, 3, part], nxt)

        @pl.when(s <= 3)
        def _():
            r = part_ref(plane, part)

            @pl.when(part == 0)
            def _():
                send(r, r, y_s.at[s - 1, side], y_r.at[s - 1, side], across)

            send(r, r, c_s.at[s - 1, side, part], c_r.at[s - 1, side, part], twin)

        @pl.when(s == 4)
        def _():
            r = part_ref(plane, part, side)

            @pl.when(part == 0)
            def _():
                send(r, r, y_s.at[3, side], y_r.at[3, side], across)

            send(r, r, c_s.at[3, side, part], c_r.at[3, side, part], twin)

        @pl.when(t == 0)
        def _():
            own_copies[2].wait()
            own_copies[3].wait()
            for x_ in xs:
                got(q_in.at[x_], qx_s.at[x_], qx_r.at[x_])
                got(doc_in.at[x_], dx_s.at[x_], dx_r.at[x_])
            for part_ in range(4):
                got(twin_ref(z, part_), c0_s.at[part_], c0_r.at[part_])
            for rb_ in range(NX):
                line = jnp.broadcast_to(doc_in[rb_].astype(F32), (HEAD, HEAD))
                line = jnp.transpose(line).astype(jnp.int32)
                line = jnp.where(rnd == 1, line[STRIPE:], line[:STRIPE])
                for g in range(GROUP):
                    q_rows[rb_, g * STRIPE:(g + 1) * STRIPE] = q_in[rb_, :, g * HEAD:(g + 1) * HEAD]
                    doc_rows[rb_, g * STRIPE:(g + 1) * STRIPE] = line
            top[...] = jnp.full(top.shape, MASKED, F32)
            acc[...] = jnp.zeros(acc.shape, F32)

        cs, rb = e // 4, e % 4

        @pl.when((s > 1) & (rb == 0))
        def _():
            back = (z + NZ - (s - 1) + 2 * (s - 1) * cs) % NZ
            for part_ in range(4):
                got(twin_ref(back, part_), c_s.at[s - 2, cs, part_], c_r.at[s - 2, cs, part_])

        chunk(s - 1, cs, rb)

        @pl.when((t % 2 == 1) & (t < 2 * NPIECE))
        def _():
            w_first(t // 2)

        @pl.when((t % 2 == 0) & (t >= WLAG) & (t < WLAG + 2 * NPIECE))
        def _():
            w_second((t - WLAG) // 2)

        return carry

    lax.fori_loop(0, 32, event, 0)

    far = (z + 4) % NZ
    for side in range(2):
        for part in range(4):
            got(twin_ref(far, part, side), c_s.at[3, side, part], c_r.at[3, side, part])

    def place(ref, x_):
        return ref.at[pl.ds(pl.multiple_of(x_ // 2 * STRIPE, STRIPE), STRIPE),
                      pl.ds(pl.multiple_of(x_ % 2 * GROUP * HEAD, HEAD), GROUP * HEAD)]

    def last(rb, carry):
        chunk(4, 0, rb)
        total = acc[rb]
        o = (total[:, :HEAD] / total[:, HEAD:]).astype(BF16)
        for g in range(GROUP):
            attn_send[rb, :, g * HEAD:(g + 1) * HEAD] = o[g * STRIPE:(g + 1) * STRIPE]

        send(attn_send.at[rb], place(attn_far, x), of_s.at[rb], of_r.at[x], dev(z, rb, y, core, 1 - h))

        @pl.when(rb != x)
        def _():
            send(attn_send.at[rb], place(attn_in, x), o_s.at[rb], o_r.at[x], dev(z, rb, y, core, h))

        return carry

    lax.fori_loop(0, NX, last, 0)
    home = pltpu.make_async_copy(attn_send.at[x], place(attn_in, x), loc_sem.at[0])
    home.start()

    for n in range(NPIECE // 2):
        w_third(n)

    def near(j, carry):
        cols = pl.ds(pl.multiple_of(j * CHUNK, CHUNK), CHUNK)
        own_part[:, cols] = jnp.dot(attn_in[...], w_own[:, cols], preferred_element_type=F32)
        return carry

    def far_too(j, carry):
        cols = pl.ds(pl.multiple_of(j * CHUNK, CHUNK), CHUNK)
        rest = jnp.dot(attn_far[...], w_far[:, cols], preferred_element_type=F32)
        out_ref[:, cols] = (own_part[:, cols] + rest).astype(BF16)
        return carry

    w_copy.wait()
    home.wait()
    for x_ in xs:
        got(place(attn_in, x_), o_s.at[x_], o_r.at[x_])
    lax.fori_loop(0, NCH, near, 0)
    for x_ in xs:
        for n in range(2):
            for d_ in range(2):
                sent(kv.at[z, x_, y, core, n], kx_s.at[d_, x_, n], kx_r.at[d_, x_, n])
        sent(q_in.at[x_], qx_s.at[x_], qx_r.at[x_])
        sent(doc_in.at[x_], dx_s.at[x_], dx_r.at[x_])
        sent(attn_send.at[x_], o_s.at[x_], o_r.at[x_])
    for part in range(4):
        sent(part_ref(z, part), c0_s.at[part], c0_r.at[part])
    for n in range(4):
        for side in range(2):
            half = side if n == 3 else None
            for part in range(3):
                sent(part_ref(z, part, half), z_s.at[side, n, part], z_r.at[side, n, part])
            for part in range(4):
                sent(part_ref(z, part, half), c_s.at[n, side, part], c_r.at[n, side, part])
            sent(part_ref(z, 0, half), y_s.at[n, side], y_r.at[n, side])
    for x_ in range(NX):
        sent(attn_send.at[x_], of_s.at[x_], of_r.at[x_])
    for i in range(NPIECE):
        ref = w_piece(x, core, i)
        sent(ref, wo_s.at[i], wo_r.at[i])
        for side in range(2):
            sent(ref, wx_s.at[side, i], wx_r.at[side, i])
        for hop in range(4):
            sent(ref, wt_s.at[hop, i], wt_r.at[hop, i])
    for n in range(NPIECE // 2):
        for side in range(2):
            sent(w_piece(x, core, n), wy_s.at[side, n], wy_r.at[side, n])
    for n in range(2):
        sent(kv.at[z, x, y, core, n], kx_s.at[1, x, n], kx_r.at[1, x, n])

    for hop, x_ in enumerate((x, left, right, (x + 2) % NX)):
        for i in range(NPIECE):
            got(w_piece(x_, 1 - core, i), wt_s.at[hop, i], wt_r.at[hop, i])
    for x_ in range(NX):
        got(place(attn_far, x_), of_s.at[x_], of_r.at[x_])
    lax.fori_loop(0, NCH, far_too, 0)


def local(queries, keys, values, doc_start, out_weight):
    docs = doc_start.reshape(1, doc_start.shape[0])
    dma = pltpu.SemaphoreType.DMA
    anyspace = pl.BlockSpec(memory_space=pl.ANY)
    return pl.pallas_call(
        kernel,
        out_shape=jax.ShapeDtypeStruct((2 * STRIPE, COLS), BF16),
        in_specs=[anyspace] * 5,
        out_specs=pl.BlockSpec(memory_space=pltpu.VMEM),
        scratch_shapes=[
            pltpu.VMEM((NZ, NX, NY, NC, 2, STRIPE, HEAD), BF16),
            pltpu.VMEM((NX, STRIPE, GROUP * HEAD), BF16),
            pltpu.VMEM((NX, 1, HEAD), jnp.int32),
            pltpu.VMEM((NX, ROWS, HEAD), BF16),
            pltpu.VMEM((NX, ROWS, HEAD), jnp.int32),
            pltpu.VMEM((NX, ROWS, HEAD), F32),
            pltpu.VMEM((NX, ROWS, 2 * HEAD), F32),
            pltpu.VMEM((NX, STRIPE, GROUP * HEAD), BF16),
            pltpu.VMEM((2 * STRIPE, 2 * GROUP * HEAD), BF16),
            pltpu.VMEM((2 * STRIPE, 2 * GROUP * HEAD), BF16),
            pltpu.VMEM((2 * GROUP * HEAD, COLS), BF16),
            pltpu.VMEM((2 * GROUP * HEAD, COLS), BF16),
            pltpu.VMEM((2 * STRIPE, COLS), F32),
            dma((4,)), dma((1,)),
            dma((2, NX, 2)), dma((2, NX, 2)), dma((NX,)), dma((NX,)), dma((NX,)), dma((NX,)),
            dma((2, 4, 3)), dma((2, 4, 3)), dma((4,)), dma((4,)), dma((4, 2, 4)), dma((4, 2, 4)),
            dma((4, 2)), dma((4, 2)), dma((NX,)), dma((NX,)),
            dma((NX,)), dma((NX,)), dma((NPIECE,)), dma((NPIECE,)), dma((2, NPIECE)), dma((2, NPIECE)),
            dma((2, NPIECE // 2)), dma((2, NPIECE // 2)), dma((4, NPIECE)), dma((4, NPIECE)),
        ],
        compiler_params=pltpu.CompilerParams(
            collective_id=0, has_side_effects=True, vmem_limit_bytes=56 * 1024 * 1024),
    )(queries, keys, values, docs, out_weight)


def solution(mesh):
    placed = (P("ctx", "head"), P("ctx", "head"), P("ctx", "head"), P("ctx"), P("head", None))
    return jax.shard_map(local, mesh=mesh, in_specs=placed, out_specs=P("ctx", "head"), check_vma=False)
```

```python
import math

import jax
import jax.numpy as jnp
from jax import lax
from jax.experimental import pallas as pl
from jax.experimental.pallas import tpu as pltpu
from jax.sharding import PartitionSpec as P

NZ, NX, NY, NC = 8, 4, 2, 2
STRIPE = 64
HEAD = 128
GROUP = 4
PLANE = NX * NY * NC * STRIPE
ROWS = GROUP * STRIPE
BLOCK = NY * NC * STRIPE
ROUND = NZ * PLANE
COLS = 2048
CHUNK = 256
NCH = COLS // CHUNK
NPIECE = 4
WROWS = 2 * GROUP * HEAD // (NX * NC * NPIECE)
WLAG = 19
PAIR = 2
MASKED = -1e30
LOG2 = math.log2(math.e) / math.sqrt(HEAD)
MESH = pl.DeviceIdType.MESH
F32 = jnp.float32
BF16 = jnp.bfloat16


def kernel(q_hbm, k_hbm, v_hbm, doc_hbm, w_hbm, out_ref,
           kv, q_in, doc_in, q_rows, doc_rows, top, acc, attn_send, attn_in, attn_far, w_own, w_far,
           own_part,
           loc_sem, w_sem, kx_s, kx_r, qx_s, qx_r, dx_s, dx_r, z_s, z_r, c0_s, c0_r, c_s, c_r,
           y_s, y_r, o_s, o_r, of_s, of_r, wo_s, wo_r, wx_s, wx_r, wy_s, wy_r, wt_s, wt_r):
    c = lax.axis_index("ctx")
    h = lax.axis_index("head")
    z, x, y, core = c // 16, (c // 4) % NX, (c // 2) % NY, c % NC
    rnd = x // 2

    def dev(z_, x_, y_, k_, h_):
        return (((z_ * NX + x_) * NY + y_) * NC + k_, h_)

    up = dev((z + 1) % NZ, x, y, core, h)
    down = dev((z + NZ - 1) % NZ, x, y, core, h)
    across = dev(z, x, 1 - y, core, h)
    twin = dev(z, x, y, 1 - core, h)
    outer = dev(z, x, 1 - y, core, 1 - h)
    right, left = (x + 1) % NX, (x + NX - 1) % NX
    xs = [(x + d) % NX for d in (2, 1, 3)]

    def send(src, dst, ss, rs, to):
        cp = pltpu.make_async_remote_copy(src, dst, ss, rs, device_id=to, device_id_type=MESH)
        cp.start()

    def got(ref, ss, rs):
        pltpu.make_async_remote_copy(ref, ref, ss, rs, device_id=twin, device_id_type=MESH).wait_recv()

    def sent(ref, ss, rs):
        pltpu.make_async_remote_copy(ref, ref, ss, rs, device_id=twin, device_id_type=MESH).wait_send()

    barrier = pltpu.get_barrier_semaphore()
    peers = [up, down, across, twin, outer] + [dev(z, x_, y, core, h) for x_ in xs]
    peers += [dev(z, x_, 1 - y, core, h) for x_ in xs]
    peers += [dev(z, x_, y, core, 1 - h) for x_ in range(NX)]
    for peer in peers:
        pl.semaphore_signal(barrier, inc=1, device_id=peer, device_id_type=MESH)

    def kv_src(ref, x_):
        return ref.at[pl.ds(pl.multiple_of(x_ // 2 * STRIPE, STRIPE), STRIPE),
                      pl.ds(pl.multiple_of(x_ % 2 * HEAD, HEAD), HEAD)]

    def q_src(x_):
        return q_hbm.at[pl.ds(pl.multiple_of(x_ // 2 * STRIPE, STRIPE), STRIPE),
                        pl.ds(pl.multiple_of(x_ % 2 * GROUP * HEAD, HEAD), GROUP * HEAD)]

    own_copies = [
        pltpu.make_async_copy(kv_src(k_hbm, x), kv.at[z, x, y, core, 0], loc_sem.at[0]),
        pltpu.make_async_copy(kv_src(v_hbm, x), kv.at[z, x, y, core, 1], loc_sem.at[1]),
        pltpu.make_async_copy(q_src(x), q_in.at[x], loc_sem.at[2]),
        pltpu.make_async_copy(doc_hbm, doc_in.at[x], loc_sem.at[3]),
    ]
    for cp in own_copies:
        cp.start()
    pl.semaphore_wait(barrier, len(peers))

    for y_, d_ in ((y, 0), (1 - y, 1)):
        for x_ in (xs if d_ == 0 else xs + [x]):
            for n, ref in enumerate((k_hbm, v_hbm)):
                send(kv_src(ref, x_), kv.at[z, x, y, core, n], kx_s.at[d_, x_, n], kx_r.at[d_, x, n],
                     dev(z, x_, y_, core, h))
    for x_ in xs:
        to = dev(z, x_, y, core, h)
        send(q_src(x_), q_in.at[x], qx_s.at[x_], qx_r.at[x], to)
        send(doc_hbm, doc_in.at[x], dx_s.at[x_], dx_r.at[x], to)

    def w_rows(x_, k_, i_):
        return pl.ds(pl.multiple_of((x_ * NC + k_) * NPIECE * WROWS + i_ * WROWS, WROWS), WROWS)

    def w_piece(x_, k_, i_):
        return w_far.at[w_rows(x_, k_, i_)]

    for i in range(NPIECE):
        send(w_hbm.at[w_rows(x, core, i), pl.ds(pl.multiple_of((1 - h) * COLS, COLS), COLS)],
             w_piece(x, core, i), wo_s.at[i], wo_r.at[i], outer)

    def w_first(i):
        ref = w_piece(x, core, i)
        got(ref, wo_s.at[i], wo_r.at[i])
        send(ref, ref, wx_s.at[0, i], wx_r.at[0, i], dev(z, right, y, core, h))
        send(ref, ref, wx_s.at[1, i], wx_r.at[1, i], dev(z, left, y, core, h))
        send(ref, ref, wt_s.at[0, i], wt_r.at[0, i], twin)

    def w_second(i):
        for side, (src, dst) in enumerate(((left, right), (right, left))):
            ref = w_piece(src, core, i)
            got(ref, wx_s.at[side, i], wx_r.at[side, i])

            @pl.when(i // (NPIECE // 2) == side)
            def _():
                n = i % (NPIECE // 2)
                send(ref, ref, wy_s.at[side, n], wy_r.at[side, n], dev(z, dst, y, core, h))

            send(ref, ref, wt_s.at[1 + side, i], wt_r.at[1 + side, i], twin)

    def w_third(n):
        for side in range(2):
            i = side * (NPIECE // 2) + n
            ref = w_piece((x + 2) % NX, core, i)
            got(ref, wy_s.at[side, n], wy_r.at[side, n])
            send(ref, ref, wt_s.at[3, i], wt_r.at[3, i], twin)

    w_copy = pltpu.make_async_copy(w_hbm.at[:, pl.ds(pl.multiple_of(h * COLS, COLS), COLS)], w_own, w_sem.at[0])

    def part_ref(zp, part, half=None):
        xb = 2 * (((part + 1) // 2 + 1) % 2)
        yy = (y + part // 2) % 2
        if half is None:
            return kv.at[zp, pl.ds(xb, 2), yy, core]
        return kv.at[zp, pl.ds(xb + half, 1), yy, core]

    def own_part_in(part):
        d_ = part // 2
        for half in range(2):
            x_ = 2 * (((part + 1) // 2 + 1) % 2) + half

            def arrive():
                for n in range(2):
                    got(kv.at[z, x_, (y + d_) % 2, core, n], kx_s.at[d_, x_, n], kx_r.at[d_, x_, n])

            if d_:
                arrive()
            else:
                pl.when(x_ != x)(arrive)

    own_copies[0].wait()
    own_copies[1].wait()
    for part in (0, 1, 2, 3):
        own_part_in(part)
        ref = part_ref(z, part)
        if part < 3:
            send(ref, ref, z_s.at[0, 0, part], z_r.at[0, 0, part], up)
            send(ref, ref, z_s.at[1, 0, part], z_r.at[1, 0, part], down)
        send(ref, ref, c0_s.at[part], c0_r.at[part], twin)
    w_copy.start()

    def twin_ref(zp, part, half=None):
        xb = 2 * (((part + 1) // 2 + 1) % 2)
        yy = (y + part // 2) % 2
        if half is None:
            return kv.at[zp, pl.ds(xb, 2), yy, 1 - core]
        return kv.at[zp, pl.ds(xb + half, 1), yy, 1 - core]

    def work(plane, base, tiles, own, docs):
        def scores(r, b):
            keys = kv[plane, b, :, :, 0].reshape(BLOCK, HEAD)
            s = lax.dot_general(q_rows[base + r], keys, (((1,), (1,)), ((), ())), preferred_element_type=F32)
            if docs:
                kpos = rnd * ROUND + plane * PLANE + b * BLOCK + lax.broadcasted_iota(jnp.int32, (ROWS, BLOCK), 1)
                seen = kpos >= jnp.tile(doc_rows[base + r], (1, BLOCK // HEAD))
                if own:
                    first = rnd * ROUND + (z * 16 + (base + r) * 4 + y * 2 + core) * STRIPE
                    qpos = first + lax.broadcasted_iota(jnp.int32, (ROWS, BLOCK), 0) % STRIPE
                    seen = seen & (kpos <= qpos)
                s = jnp.where(seen, s, MASKED)
            return s

        s = scores(*tiles[0])
        for n, (r, b) in enumerate(tiles):
            ahead = scores(*tiles[n + 1]) if n + 1 < len(tiles) else None
            if b == 0:
                old, total = top[base + r], acc[base + r]
            new = jnp.maximum(old, jnp.max(s, axis=1, keepdims=True))
            p = jnp.exp2(s * LOG2 - jnp.tile(new * LOG2, (1, BLOCK // HEAD))).astype(BF16)
            shrink = jnp.exp2((old - new) * LOG2)
            values = kv[plane, b, :, :, 1].reshape(BLOCK, HEAD)
            both = jnp.concatenate([values, jnp.ones((BLOCK, HEAD), BF16)], axis=1)
            total = total * jnp.tile(shrink, (1, 2)) + jnp.dot(p, both, preferred_element_type=F32)
            old, s = new, ahead
            if n + 1 == len(tiles) or tiles[n + 1][0] != r:
                acc[base + r] = total
                top[base + r] = old

    every = [(r, b) for r in range(PAIR) for b in range(NX)]

    def chunk(d, side, pair):
        plane = (z + NZ - d + 2 * d * side) % NZ
        earlier = (d > 0) & (plane < z)
        for n in range(NX // PAIR):
            @pl.when((d == 0) & (side == 0) & (pair == n))
            def _():
                work(z, n * PAIR, [(r, b) for r, b in every if b <= n * PAIR + r], True, True)

        @pl.when(earlier & (rnd == 1))
        def _():
            work(plane, pair * PAIR, every, False, True)

        @pl.when(earlier & (rnd == 0))
        def _():
            work(plane, pair * PAIR, every, False, False)

    def event(t, carry):
        s = t // 8 + 1
        e = t % 8
        side, part = e % 2, e // 2
        plane = (z + NZ - s + 2 * s * side) % NZ
        nxt = dev((z + 1 + (NZ - 2) * side) % NZ, x, y, core, h)

        @pl.when((s <= 3) & (part <= 2))
        def _():
            got(part_ref(plane, part), z_s.at[side, s - 1, part], z_r.at[side, s - 1, part])

        @pl.when((s == 4) & (part <= 2))
        def _():
            got(part_ref(plane, part, side), z_s.at[side, 3, part], z_r.at[side, 3, part])

        @pl.when((s <= 3) & (part == 3))
        def _():
            got(part_ref(plane, 3), y_s.at[s - 1, side], y_r.at[s - 1, side])

        @pl.when((s == 4) & (part == 3))
        def _():
            got(part_ref(plane, 3, side), y_s.at[3, side], y_r.at[3, side])

        @pl.when((s <= 2) & (part <= 2))
        def _():
            r = part_ref(plane, part)
            send(r, r, z_s.at[side, s, part], z_r.at[side, s, part], nxt)

        @pl.when((s == 3) & (part <= 2))
        def _():
            r = part_ref(plane, part, side)
            send(r, r, z_s.at[side, 3, part], z_r.at[side, 3, part], nxt)

        @pl.when(s <= 3)
        def _():
            r = part_ref(plane, part)

            @pl.when(part == 0)
            def _():
                send(r, r, y_s.at[s - 1, side], y_r.at[s - 1, side], across)

            send(r, r, c_s.at[s - 1, side, part], c_r.at[s - 1, side, part], twin)

        @pl.when(s == 4)
        def _():
            r = part_ref(plane, part, side)

            @pl.when(part == 0)
            def _():
                send(r, r, y_s.at[3, side], y_r.at[3, side], across)

            send(r, r, c_s.at[3, side, part], c_r.at[3, side, part], twin)

        @pl.when(t == 0)
        def _():
            own_copies[2].wait()
            own_copies[3].wait()
            for x_ in xs:
                got(q_in.at[x_], qx_s.at[x_], qx_r.at[x_])
                got(doc_in.at[x_], dx_s.at[x_], dx_r.at[x_])
            for part_ in range(4):
                got(twin_ref(z, part_), c0_s.at[part_], c0_r.at[part_])
            for rb_ in range(NX):
                line = jnp.broadcast_to(doc_in[rb_].astype(F32), (HEAD, HEAD))
                line = jnp.transpose(line).astype(jnp.int32)
                line = jnp.where(rnd == 1, line[STRIPE:], line[:STRIPE])
                for g in range(GROUP):
                    q_rows[rb_, g * STRIPE:(g + 1) * STRIPE] = q_in[rb_, :, g * HEAD:(g + 1) * HEAD]
                    doc_rows[rb_, g * STRIPE:(g + 1) * STRIPE] = line
            top[...] = jnp.full(top.shape, MASKED, F32)
            acc[...] = jnp.zeros(acc.shape, F32)

        @pl.when(e % 2 == 0)
        def _():
            cs, pair = e // 4, (e // 2) % 2

            @pl.when((s > 1) & (pair == 0))
            def _():
                back = (z + NZ - (s - 1) + 2 * (s - 1) * cs) % NZ
                for part_ in range(4):
                    got(twin_ref(back, part_), c_s.at[s - 2, cs, part_], c_r.at[s - 2, cs, part_])

            chunk(s - 1, cs, pair)

        @pl.when((t % 2 == 1) & (t < 2 * NPIECE))
        def _():
            w_first(t // 2)

        @pl.when((t % 2 == 1) & (t >= WLAG) & (t < WLAG + 2 * NPIECE))
        def _():
            w_second((t - WLAG) // 2)

        return carry

    lax.fori_loop(0, 32, event, 0)

    far = (z + 4) % NZ
    for side in range(2):
        for part in range(4):
            got(twin_ref(far, part, side), c_s.at[3, side, part], c_r.at[3, side, part])

    def place(ref, x_):
        return ref.at[pl.ds(pl.multiple_of(x_ // 2 * STRIPE, STRIPE), STRIPE),
                      pl.ds(pl.multiple_of(x_ % 2 * GROUP * HEAD, HEAD), GROUP * HEAD)]

    def last(pair, carry):
        chunk(4, 0, pair)

        def finish(r, inner):
            rb = pair * PAIR + r
            total = acc[rb]
            o = (total[:, :HEAD] / total[:, HEAD:]).astype(BF16)
            for g in range(GROUP):
                attn_send[rb, :, g * HEAD:(g + 1) * HEAD] = o[g * STRIPE:(g + 1) * STRIPE]
            send(attn_send.at[rb], place(attn_far, x), of_s.at[rb], of_r.at[x], dev(z, rb, y, core, 1 - h))

            @pl.when(rb != x)
            def _():
                send(attn_send.at[rb], place(attn_in, x), o_s.at[rb], o_r.at[x], dev(z, rb, y, core, h))

            return inner

        return lax.fori_loop(0, PAIR, finish, carry)

    lax.fori_loop(0, NX // PAIR, last, 0)
    home = pltpu.make_async_copy(attn_send.at[x], place(attn_in, x), loc_sem.at[0])
    home.start()

    for n in range(NPIECE // 2):
        w_third(n)

    def near(j, carry):
        cols = pl.ds(pl.multiple_of(j * CHUNK, CHUNK), CHUNK)
        own_part[:, cols] = jnp.dot(attn_in[...], w_own[:, cols], preferred_element_type=F32)
        return carry

    def far_too(j, carry):
        cols = pl.ds(pl.multiple_of(j * CHUNK, CHUNK), CHUNK)
        rest = jnp.dot(attn_far[...], w_far[:, cols], preferred_element_type=F32)
        out_ref[:, cols] = (own_part[:, cols] + rest).astype(BF16)
        return carry

    w_copy.wait()
    home.wait()
    for x_ in xs:
        got(place(attn_in, x_), o_s.at[x_], o_r.at[x_])
    lax.fori_loop(0, NCH, near, 0)
    for x_ in xs:
        for n in range(2):
            for d_ in range(2):
                sent(kv.at[z, x_, y, core, n], kx_s.at[d_, x_, n], kx_r.at[d_, x_, n])
        sent(q_in.at[x_], qx_s.at[x_], qx_r.at[x_])
        sent(doc_in.at[x_], dx_s.at[x_], dx_r.at[x_])
        sent(attn_send.at[x_], o_s.at[x_], o_r.at[x_])
    for part in range(4):
        sent(part_ref(z, part), c0_s.at[part], c0_r.at[part])
    for n in range(4):
        for side in range(2):
            half = side if n == 3 else None
            for part in range(3):
                sent(part_ref(z, part, half), z_s.at[side, n, part], z_r.at[side, n, part])
            for part in range(4):
                sent(part_ref(z, part, half), c_s.at[n, side, part], c_r.at[n, side, part])
            sent(part_ref(z, 0, half), y_s.at[n, side], y_r.at[n, side])
    for x_ in range(NX):
        sent(attn_send.at[x_], of_s.at[x_], of_r.at[x_])
    for i in range(NPIECE):
        ref = w_piece(x, core, i)
        sent(ref, wo_s.at[i], wo_r.at[i])
        for side in range(2):
            sent(ref, wx_s.at[side, i], wx_r.at[side, i])
        for hop in range(4):
            sent(ref, wt_s.at[hop, i], wt_r.at[hop, i])
    for n in range(NPIECE // 2):
        for side in range(2):
            sent(w_piece(x, core, n), wy_s.at[side, n], wy_r.at[side, n])
    for n in range(2):
        sent(kv.at[z, x, y, core, n], kx_s.at[1, x, n], kx_r.at[1, x, n])

    for hop, x_ in enumerate((x, left, right, (x + 2) % NX)):
        for i in range(NPIECE):
            got(w_piece(x_, 1 - core, i), wt_s.at[hop, i], wt_r.at[hop, i])
    for x_ in range(NX):
        got(place(attn_far, x_), of_s.at[x_], of_r.at[x_])
    lax.fori_loop(0, NCH, far_too, 0)


def local(queries, keys, values, doc_start, out_weight):
    docs = doc_start.reshape(1, doc_start.shape[0])
    dma = pltpu.SemaphoreType.DMA
    anyspace = pl.BlockSpec(memory_space=pl.ANY)
    return pl.pallas_call(
        kernel,
        out_shape=jax.ShapeDtypeStruct((2 * STRIPE, COLS), BF16),
        in_specs=[anyspace] * 5,
        out_specs=pl.BlockSpec(memory_space=pltpu.VMEM),
        scratch_shapes=[
            pltpu.VMEM((NZ, NX, NY, NC, 2, STRIPE, HEAD), BF16),
            pltpu.VMEM((NX, STRIPE, GROUP * HEAD), BF16),
            pltpu.VMEM((NX, 1, HEAD), jnp.int32),
            pltpu.VMEM((NX, ROWS, HEAD), BF16),
            pltpu.VMEM((NX, ROWS, HEAD), jnp.int32),
            pltpu.VMEM((NX, ROWS, HEAD), F32),
            pltpu.VMEM((NX, ROWS, 2 * HEAD), F32),
            pltpu.VMEM((NX, STRIPE, GROUP * HEAD), BF16),
            pltpu.VMEM((2 * STRIPE, 2 * GROUP * HEAD), BF16),
            pltpu.VMEM((2 * STRIPE, 2 * GROUP * HEAD), BF16),
            pltpu.VMEM((2 * GROUP * HEAD, COLS), BF16),
            pltpu.VMEM((2 * GROUP * HEAD, COLS), BF16),
            pltpu.VMEM((2 * STRIPE, COLS), F32),
            dma((4,)), dma((1,)),
            dma((2, NX, 2)), dma((2, NX, 2)), dma((NX,)), dma((NX,)), dma((NX,)), dma((NX,)),
            dma((2, 4, 3)), dma((2, 4, 3)), dma((4,)), dma((4,)), dma((4, 2, 4)), dma((4, 2, 4)),
            dma((4, 2)), dma((4, 2)), dma((NX,)), dma((NX,)),
            dma((NX,)), dma((NX,)), dma((NPIECE,)), dma((NPIECE,)), dma((2, NPIECE)), dma((2, NPIECE)),
            dma((2, NPIECE // 2)), dma((2, NPIECE // 2)), dma((4, NPIECE)), dma((4, NPIECE)),
        ],
        compiler_params=pltpu.CompilerParams(
            collective_id=0, has_side_effects=True, vmem_limit_bytes=56 * 1024 * 1024),
    )(queries, keys, values, docs, out_weight)


def solution(mesh):
    placed = (P("ctx", "head"), P("ctx", "head"), P("ctx", "head"), P("ctx"), P("head", None))
    return jax.shard_map(local, mesh=mesh, in_specs=placed, out_specs=P("ctx", "head"), check_vma=False)
```

```python
import math

import jax
import jax.numpy as jnp
from jax import lax
from jax.experimental import pallas as pl
from jax.experimental.pallas import tpu as pltpu
from jax.sharding import PartitionSpec as P

NZ, NX, NY, NC = 8, 4, 2, 2
STRIPE = 64
HEAD = 128
GROUP = 4
PLANE = NX * NY * NC * STRIPE
ROWS = GROUP * STRIPE
BLOCK = NY * NC * STRIPE
ROUND = NZ * PLANE
COLS = 2048
CHUNK = 2048
NCH = COLS // CHUNK
NPIECE = 4
WROWS = 2 * GROUP * HEAD // (NX * NC * NPIECE)
WLAG = 19
PAIR = 2
MASKED = -1e30
LOG2 = math.log2(math.e) / math.sqrt(HEAD)
MESH = pl.DeviceIdType.MESH
F32 = jnp.float32
BF16 = jnp.bfloat16


def kernel(q_hbm, k_hbm, v_hbm, doc_hbm, w_hbm, out_ref,
           kv, q_in, doc_in, q_rows, doc_rows, top, acc, attn_send, attn_in, attn_far, w_own, w_far,
           own_part,
           loc_sem, w_sem, kx_s, kx_r, qx_s, qx_r, dx_s, dx_r, z_s, z_r, c0_s, c0_r, c_s, c_r,
           y_s, y_r, o_s, o_r, of_s, of_r, wo_s, wo_r, wx_s, wx_r, wy_s, wy_r, wt_s, wt_r):
    c = lax.axis_index("ctx")
    h = lax.axis_index("head")
    z, x, y, core = c // 16, (c // 4) % NX, (c // 2) % NY, c % NC
    rnd = x // 2

    def dev(z_, x_, y_, k_, h_):
        return (((z_ * NX + x_) * NY + y_) * NC + k_, h_)

    up = dev((z + 1) % NZ, x, y, core, h)
    down = dev((z + NZ - 1) % NZ, x, y, core, h)
    across = dev(z, x, 1 - y, core, h)
    twin = dev(z, x, y, 1 - core, h)
    outer = dev(z, x, 1 - y, core, 1 - h)
    right, left = (x + 1) % NX, (x + NX - 1) % NX
    xs = [(x + d) % NX for d in (2, 1, 3)]

    def send(src, dst, ss, rs, to):
        cp = pltpu.make_async_remote_copy(src, dst, ss, rs, device_id=to, device_id_type=MESH)
        cp.start()

    def got(ref, ss, rs):
        pltpu.make_async_remote_copy(ref, ref, ss, rs, device_id=twin, device_id_type=MESH).wait_recv()

    def sent(ref, ss, rs):
        pltpu.make_async_remote_copy(ref, ref, ss, rs, device_id=twin, device_id_type=MESH).wait_send()

    barrier = pltpu.get_barrier_semaphore()
    peers = [up, down, across, twin, outer] + [dev(z, x_, y, core, h) for x_ in xs]
    peers += [dev(z, x_, 1 - y, core, h) for x_ in xs]
    peers += [dev(z, x_, y, core, 1 - h) for x_ in range(NX)]
    for peer in peers:
        pl.semaphore_signal(barrier, inc=1, device_id=peer, device_id_type=MESH)

    def kv_src(ref, x_):
        return ref.at[pl.ds(pl.multiple_of(x_ // 2 * STRIPE, STRIPE), STRIPE),
                      pl.ds(pl.multiple_of(x_ % 2 * HEAD, HEAD), HEAD)]

    def q_src(x_):
        return q_hbm.at[pl.ds(pl.multiple_of(x_ // 2 * STRIPE, STRIPE), STRIPE),
                        pl.ds(pl.multiple_of(x_ % 2 * GROUP * HEAD, HEAD), GROUP * HEAD)]

    own_copies = [
        pltpu.make_async_copy(kv_src(k_hbm, x), kv.at[z, x, y, core, 0], loc_sem.at[0]),
        pltpu.make_async_copy(kv_src(v_hbm, x), kv.at[z, x, y, core, 1], loc_sem.at[1]),
        pltpu.make_async_copy(q_src(x), q_in.at[x], loc_sem.at[2]),
        pltpu.make_async_copy(doc_hbm, doc_in.at[x], loc_sem.at[3]),
    ]
    for cp in own_copies:
        cp.start()
    pl.semaphore_wait(barrier, len(peers))

    for y_, d_ in ((y, 0), (1 - y, 1)):
        for x_ in (xs if d_ == 0 else xs + [x]):
            for n, ref in enumerate((k_hbm, v_hbm)):
                send(kv_src(ref, x_), kv.at[z, x, y, core, n], kx_s.at[d_, x_, n], kx_r.at[d_, x, n],
                     dev(z, x_, y_, core, h))
    for x_ in xs:
        to = dev(z, x_, y, core, h)
        send(q_src(x_), q_in.at[x], qx_s.at[x_], qx_r.at[x], to)
        send(doc_hbm, doc_in.at[x], dx_s.at[x_], dx_r.at[x], to)

    def w_rows(x_, k_, i_):
        return pl.ds(pl.multiple_of((x_ * NC + k_) * NPIECE * WROWS + i_ * WROWS, WROWS), WROWS)

    def w_piece(x_, k_, i_):
        return w_far.at[w_rows(x_, k_, i_)]

    for i in range(NPIECE):
        send(w_hbm.at[w_rows(x, core, i), pl.ds(pl.multiple_of((1 - h) * COLS, COLS), COLS)],
             w_piece(x, core, i), wo_s.at[i], wo_r.at[i], outer)

    def w_first(i):
        ref = w_piece(x, core, i)
        got(ref, wo_s.at[i], wo_r.at[i])
        send(ref, ref, wx_s.at[0, i], wx_r.at[0, i], dev(z, right, y, core, h))
        send(ref, ref, wx_s.at[1, i], wx_r.at[1, i], dev(z, left, y, core, h))
        send(ref, ref, wt_s.at[0, i], wt_r.at[0, i], twin)

    def w_second(i):
        for side, (src, dst) in enumerate(((left, right), (right, left))):
            ref = w_piece(src, core, i)
            got(ref, wx_s.at[side, i], wx_r.at[side, i])

            @pl.when(i // (NPIECE // 2) == side)
            def _():
                n = i % (NPIECE // 2)
                send(ref, ref, wy_s.at[side, n], wy_r.at[side, n], dev(z, dst, y, core, h))

            send(ref, ref, wt_s.at[1 + side, i], wt_r.at[1 + side, i], twin)

    def w_third(n):
        for side in range(2):
            i = side * (NPIECE // 2) + n
            ref = w_piece((x + 2) % NX, core, i)
            got(ref, wy_s.at[side, n], wy_r.at[side, n])
            send(ref, ref, wt_s.at[3, i], wt_r.at[3, i], twin)

    w_copy = pltpu.make_async_copy(w_hbm.at[:, pl.ds(pl.multiple_of(h * COLS, COLS), COLS)], w_own, w_sem.at[0])

    def part_ref(zp, part, half=None):
        xb = 2 * (((part + 1) // 2 + 1) % 2)
        yy = (y + part // 2) % 2
        if half is None:
            return kv.at[zp, pl.ds(xb, 2), yy, core]
        return kv.at[zp, pl.ds(xb + half, 1), yy, core]

    def own_part_in(part):
        d_ = part // 2
        for half in range(2):
            x_ = 2 * (((part + 1) // 2 + 1) % 2) + half

            def arrive():
                for n in range(2):
                    got(kv.at[z, x_, (y + d_) % 2, core, n], kx_s.at[d_, x_, n], kx_r.at[d_, x_, n])

            if d_:
                arrive()
            else:
                pl.when(x_ != x)(arrive)

    own_copies[0].wait()
    own_copies[1].wait()
    for part in (0, 1, 2, 3):
        own_part_in(part)
        ref = part_ref(z, part)
        if part < 3:
            send(ref, ref, z_s.at[0, 0, part], z_r.at[0, 0, part], up)
            send(ref, ref, z_s.at[1, 0, part], z_r.at[1, 0, part], down)
        send(ref, ref, c0_s.at[part], c0_r.at[part], twin)
    w_copy.start()

    def twin_ref(zp, part, half=None):
        xb = 2 * (((part + 1) // 2 + 1) % 2)
        yy = (y + part // 2) % 2
        if half is None:
            return kv.at[zp, pl.ds(xb, 2), yy, 1 - core]
        return kv.at[zp, pl.ds(xb + half, 1), yy, 1 - core]

    def work(plane, base, tiles, own, docs):
        def scores(r, b):
            keys = kv[plane, b, :, :, 0].reshape(BLOCK, HEAD)
            s = lax.dot_general(q_rows[base + r], keys, (((1,), (1,)), ((), ())), preferred_element_type=F32)
            if docs:
                kpos = rnd * ROUND + plane * PLANE + b * BLOCK + lax.broadcasted_iota(jnp.int32, (ROWS, BLOCK), 1)
                seen = kpos >= jnp.tile(doc_rows[base + r], (1, BLOCK // HEAD))
                if own:
                    first = rnd * ROUND + (z * 16 + (base + r) * 4 + y * 2 + core) * STRIPE
                    qpos = first + lax.broadcasted_iota(jnp.int32, (ROWS, BLOCK), 0) % STRIPE
                    seen = seen & (kpos <= qpos)
                s = jnp.where(seen, s, MASKED)
            return s

        s = scores(*tiles[0])
        for n, (r, b) in enumerate(tiles):
            ahead = scores(*tiles[n + 1]) if n + 1 < len(tiles) else None
            if b == 0 and own:
                old, total = jnp.full((ROWS, HEAD), MASKED, F32), jnp.zeros((ROWS, 2 * HEAD), F32)
            elif b == 0:
                old, total = top[base + r], acc[base + r]
            new = jnp.maximum(old, jnp.max(s, axis=1, keepdims=True))
            p = jnp.exp2(s * LOG2 - jnp.tile(new * LOG2, (1, BLOCK // HEAD))).astype(BF16)
            shrink = jnp.exp2((old - new) * LOG2)
            values = kv[plane, b, :, :, 1].reshape(BLOCK, HEAD)
            both = jnp.concatenate([values, jnp.ones((BLOCK, HEAD), BF16)], axis=1)
            total = total * jnp.tile(shrink, (1, 2)) + jnp.dot(p, both, preferred_element_type=F32)
            old, s = new, ahead
            if n + 1 == len(tiles) or tiles[n + 1][0] != r:
                acc[base + r] = total
                top[base + r] = old

    every = [(r, b) for r in range(PAIR) for b in range(NX)]

    def chunk(d, side, pair):
        plane = (z + NZ - d + 2 * d * side) % NZ
        earlier = (d > 0) & (plane < z)
        for n in range(NX // PAIR):
            @pl.when((d == 0) & (side == 0) & (pair == n))
            def _():
                work(z, n * PAIR, [(r, b) for r, b in every if b <= n * PAIR + r], True, True)

        @pl.when(earlier & (rnd == 1))
        def _():
            work(plane, pair * PAIR, every, False, True)

        @pl.when(earlier & (rnd == 0))
        def _():
            work(plane, pair * PAIR, every, False, False)

    def event(t, carry):
        s = t // 8 + 1
        e = t % 8
        side, part = e % 2, e // 2
        plane = (z + NZ - s + 2 * s * side) % NZ
        nxt = dev((z + 1 + (NZ - 2) * side) % NZ, x, y, core, h)

        @pl.when((s <= 3) & (part <= 2))
        def _():
            got(part_ref(plane, part), z_s.at[side, s - 1, part], z_r.at[side, s - 1, part])

        @pl.when((s == 4) & (part <= 2))
        def _():
            got(part_ref(plane, part, side), z_s.at[side, 3, part], z_r.at[side, 3, part])

        @pl.when((s <= 3) & (part == 3))
        def _():
            got(part_ref(plane, 3), y_s.at[s - 1, side], y_r.at[s - 1, side])

        @pl.when((s == 4) & (part == 3))
        def _():
            got(part_ref(plane, 3, side), y_s.at[3, side], y_r.at[3, side])

        @pl.when((s <= 2) & (part <= 2))
        def _():
            r = part_ref(plane, part)
            send(r, r, z_s.at[side, s, part], z_r.at[side, s, part], nxt)

        @pl.when((s == 3) & (part <= 2))
        def _():
            r = part_ref(plane, part, side)
            send(r, r, z_s.at[side, 3, part], z_r.at[side, 3, part], nxt)

        @pl.when(s <= 3)
        def _():
            r = part_ref(plane, part)

            @pl.when(part == 0)
            def _():
                send(r, r, y_s.at[s - 1, side], y_r.at[s - 1, side], across)

            send(r, r, c_s.at[s - 1, side, part], c_r.at[s - 1, side, part], twin)

        @pl.when(s == 4)
        def _():
            r = part_ref(plane, part, side)

            @pl.when(part == 0)
            def _():
                send(r, r, y_s.at[3, side], y_r.at[3, side], across)

            send(r, r, c_s.at[3, side, part], c_r.at[3, side, part], twin)

        @pl.when(t == 0)
        def _():
            own_copies[2].wait()
            own_copies[3].wait()
            for x_ in xs:
                got(q_in.at[x_], qx_s.at[x_], qx_r.at[x_])
                got(doc_in.at[x_], dx_s.at[x_], dx_r.at[x_])
            for part_ in range(4):
                got(twin_ref(z, part_), c0_s.at[part_], c0_r.at[part_])
            for rb_ in range(NX):
                line = jnp.broadcast_to(doc_in[rb_].astype(F32), (HEAD, HEAD))
                line = jnp.transpose(line).astype(jnp.int32)
                line = jnp.where(rnd == 1, line[STRIPE:], line[:STRIPE])
                for g in range(GROUP):
                    q_rows[rb_, g * STRIPE:(g + 1) * STRIPE] = q_in[rb_, :, g * HEAD:(g + 1) * HEAD]
                    doc_rows[rb_, g * STRIPE:(g + 1) * STRIPE] = line

        @pl.when(e % 2 == 0)
        def _():
            cs, pair = e // 4, (e // 2) % 2

            @pl.when((s > 1) & (pair == 0))
            def _():
                back = (z + NZ - (s - 1) + 2 * (s - 1) * cs) % NZ
                for part_ in range(4):
                    got(twin_ref(back, part_), c_s.at[s - 2, cs, part_], c_r.at[s - 2, cs, part_])

            chunk(s - 1, cs, pair)

        @pl.when((t % 2 == 1) & (t < 2 * NPIECE))
        def _():
            w_first(t // 2)

        @pl.when((t % 2 == 1) & (t >= WLAG) & (t < WLAG + 2 * NPIECE))
        def _():
            w_second((t - WLAG) // 2)

        return carry

    lax.fori_loop(0, 32, event, 0)

    far = (z + 4) % NZ
    for side in range(2):
        for part in range(4):
            got(twin_ref(far, part, side), c_s.at[3, side, part], c_r.at[3, side, part])

    def place(ref, x_):
        return ref.at[pl.ds(pl.multiple_of(x_ // 2 * STRIPE, STRIPE), STRIPE),
                      pl.ds(pl.multiple_of(x_ % 2 * GROUP * HEAD, HEAD), GROUP * HEAD)]

    def last(pair, carry):
        chunk(4, 0, pair)

        def finish(r, inner):
            rb = pair * PAIR + r
            total = acc[rb]
            o = (total[:, :HEAD] / total[:, HEAD:]).astype(BF16)
            for g in range(GROUP):
                attn_send[rb, :, g * HEAD:(g + 1) * HEAD] = o[g * STRIPE:(g + 1) * STRIPE]
            send(attn_send.at[rb], place(attn_far, x), of_s.at[rb], of_r.at[x], dev(z, rb, y, core, 1 - h))

            @pl.when(rb != x)
            def _():
                send(attn_send.at[rb], place(attn_in, x), o_s.at[rb], o_r.at[x], dev(z, rb, y, core, h))

            return inner

        return lax.fori_loop(0, PAIR, finish, carry)

    lax.fori_loop(0, NX // PAIR, last, 0)
    home = pltpu.make_async_copy(attn_send.at[x], place(attn_in, x), loc_sem.at[0])
    home.start()

    for n in range(NPIECE // 2):
        w_third(n)

    def near(j, carry):
        cols = pl.ds(pl.multiple_of(j * CHUNK, CHUNK), CHUNK)
        own_part[:, cols] = jnp.dot(attn_in[...], w_own[:, cols], preferred_element_type=F32)
        return carry

    def far_too(j, carry):
        cols = pl.ds(pl.multiple_of(j * CHUNK, CHUNK), CHUNK)
        rest = jnp.dot(attn_far[...], w_far[:, cols], preferred_element_type=F32)
        out_ref[:, cols] = (own_part[:, cols] + rest).astype(BF16)
        return carry

    w_copy.wait()
    home.wait()
    for x_ in xs:
        got(place(attn_in, x_), o_s.at[x_], o_r.at[x_])
    lax.fori_loop(0, NCH, near, 0)
    for x_ in xs:
        for n in range(2):
            for d_ in range(2):
                sent(kv.at[z, x_, y, core, n], kx_s.at[d_, x_, n], kx_r.at[d_, x_, n])
        sent(q_in.at[x_], qx_s.at[x_], qx_r.at[x_])
        sent(doc_in.at[x_], dx_s.at[x_], dx_r.at[x_])
        sent(attn_send.at[x_], o_s.at[x_], o_r.at[x_])
    for part in range(4):
        sent(part_ref(z, part), c0_s.at[part], c0_r.at[part])
    for n in range(4):
        for side in range(2):
            half = side if n == 3 else None
            for part in range(3):
                sent(part_ref(z, part, half), z_s.at[side, n, part], z_r.at[side, n, part])
            for part in range(4):
                sent(part_ref(z, part, half), c_s.at[n, side, part], c_r.at[n, side, part])
            sent(part_ref(z, 0, half), y_s.at[n, side], y_r.at[n, side])
    for x_ in range(NX):
        sent(attn_send.at[x_], of_s.at[x_], of_r.at[x_])
    for i in range(NPIECE):
        ref = w_piece(x, core, i)
        sent(ref, wo_s.at[i], wo_r.at[i])
        for side in range(2):
            sent(ref, wx_s.at[side, i], wx_r.at[side, i])
        for hop in range(4):
            sent(ref, wt_s.at[hop, i], wt_r.at[hop, i])
    for n in range(NPIECE // 2):
        for side in range(2):
            sent(w_piece(x, core, n), wy_s.at[side, n], wy_r.at[side, n])
    for n in range(2):
        sent(kv.at[z, x, y, core, n], kx_s.at[1, x, n], kx_r.at[1, x, n])

    for hop, x_ in enumerate((x, left, right, (x + 2) % NX)):
        for i in range(NPIECE):
            got(w_piece(x_, 1 - core, i), wt_s.at[hop, i], wt_r.at[hop, i])
    for x_ in range(NX):
        got(place(attn_far, x_), of_s.at[x_], of_r.at[x_])
    lax.fori_loop(0, NCH, far_too, 0)


def local(queries, keys, values, doc_start, out_weight):
    docs = doc_start.reshape(1, doc_start.shape[0])
    dma = pltpu.SemaphoreType.DMA
    anyspace = pl.BlockSpec(memory_space=pl.ANY)
    return pl.pallas_call(
        kernel,
        out_shape=jax.ShapeDtypeStruct((2 * STRIPE, COLS), BF16),
        in_specs=[anyspace] * 5,
        out_specs=pl.BlockSpec(memory_space=pltpu.VMEM),
        scratch_shapes=[
            pltpu.VMEM((NZ, NX, NY, NC, 2, STRIPE, HEAD), BF16),
            pltpu.VMEM((NX, STRIPE, GROUP * HEAD), BF16),
            pltpu.VMEM((NX, 1, HEAD), jnp.int32),
            pltpu.VMEM((NX, ROWS, HEAD), BF16),
            pltpu.VMEM((NX, ROWS, HEAD), jnp.int32),
            pltpu.VMEM((NX, ROWS, HEAD), F32),
            pltpu.VMEM((NX, ROWS, 2 * HEAD), F32),
            pltpu.VMEM((NX, STRIPE, GROUP * HEAD), BF16),
            pltpu.VMEM((2 * STRIPE, 2 * GROUP * HEAD), BF16),
            pltpu.VMEM((2 * STRIPE, 2 * GROUP * HEAD), BF16),
            pltpu.VMEM((2 * GROUP * HEAD, COLS), BF16),
            pltpu.VMEM((2 * GROUP * HEAD, COLS), BF16),
            pltpu.VMEM((2 * STRIPE, COLS), F32),
            dma((4,)), dma((1,)),
            dma((2, NX, 2)), dma((2, NX, 2)), dma((NX,)), dma((NX,)), dma((NX,)), dma((NX,)),
            dma((2, 4, 3)), dma((2, 4, 3)), dma((4,)), dma((4,)), dma((4, 2, 4)), dma((4, 2, 4)),
            dma((4, 2)), dma((4, 2)), dma((NX,)), dma((NX,)),
            dma((NX,)), dma((NX,)), dma((NPIECE,)), dma((NPIECE,)), dma((2, NPIECE)), dma((2, NPIECE)),
            dma((2, NPIECE // 2)), dma((2, NPIECE // 2)), dma((4, NPIECE)), dma((4, NPIECE)),
        ],
        compiler_params=pltpu.CompilerParams(
            collective_id=0, has_side_effects=True, vmem_limit_bytes=56 * 1024 * 1024),
    )(queries, keys, values, docs, out_weight)


def solution(mesh):
    placed = (P("ctx", "head"), P("ctx", "head"), P("ctx", "head"), P("ctx"), P("head", None))
    return jax.shard_map(local, mesh=mesh, in_specs=placed, out_specs=P("ctx", "head"), check_vma=False)
```

```python
import math

import jax
import jax.numpy as jnp
from jax import lax
from jax.experimental import pallas as pl
from jax.experimental.pallas import tpu as pltpu
from jax.sharding import PartitionSpec as P

NZ, NX, NY, NC = 8, 4, 2, 2
STRIPE = 64
HEAD = 128
GROUP = 4
PLANE = NX * NY * NC * STRIPE
ROWS = GROUP * STRIPE
BLOCK = NY * NC * STRIPE
ROUND = NZ * PLANE
COLS = 2048
CHUNK = 2048
NCH = COLS // CHUNK
NPIECE = 4
WROWS = 2 * GROUP * HEAD // (NX * NC * NPIECE)
WLAG = 19
PAIR = 2
MASKED = -1e30
LOG2 = math.log2(math.e) / math.sqrt(HEAD)
MESH = pl.DeviceIdType.MESH
F32 = jnp.float32
BF16 = jnp.bfloat16


def kernel(q_hbm, k_hbm, v_hbm, doc_hbm, w_hbm, out_ref,
           kv, q_in, doc_in, q_rows, doc_rows, top, acc, attn_send, attn_in, attn_far, w_own, w_far,
           own_part,
           loc_sem, w_sem, kx_s, kx_r, qx_s, qx_r, dx_s, dx_r, z_s, z_r, c0_s, c0_r, c_s, c_r,
           y_s, y_r, o_s, o_r, of_s, of_r, wo_s, wo_r, wx_s, wx_r, wy_s, wy_r, wt_s, wt_r):
    c = lax.axis_index("ctx")
    h = lax.axis_index("head")
    z, x, y, core = c // 16, (c // 4) % NX, (c // 2) % NY, c % NC
    rnd = x // 2

    def dev(z_, x_, y_, k_, h_):
        return (((z_ * NX + x_) * NY + y_) * NC + k_, h_)

    up = dev((z + 1) % NZ, x, y, core, h)
    down = dev((z + NZ - 1) % NZ, x, y, core, h)
    across = dev(z, x, 1 - y, core, h)
    twin = dev(z, x, y, 1 - core, h)
    outer = dev(z, x, 1 - y, core, 1 - h)
    right, left = (x + 1) % NX, (x + NX - 1) % NX
    xs = [(x + d) % NX for d in (2, 1, 3)]

    def send(src, dst, ss, rs, to):
        cp = pltpu.make_async_remote_copy(src, dst, ss, rs, device_id=to, device_id_type=MESH)
        cp.start()

    def got(ref, ss, rs):
        pltpu.make_async_remote_copy(ref, ref, ss, rs, device_id=twin, device_id_type=MESH).wait_recv()

    def sent(ref, ss, rs):
        pltpu.make_async_remote_copy(ref, ref, ss, rs, device_id=twin, device_id_type=MESH).wait_send()

    barrier = pltpu.get_barrier_semaphore()
    peers = [up, down, across, twin, outer] + [dev(z, x_, y, core, h) for x_ in xs]
    peers += [dev(z, x_, 1 - y, core, h) for x_ in xs]
    peers += [dev(z, x_, y, core, 1 - h) for x_ in range(NX)]
    for peer in peers:
        pl.semaphore_signal(barrier, inc=1, device_id=peer, device_id_type=MESH)

    def kv_src(ref, x_):
        return ref.at[pl.ds(pl.multiple_of(x_ // 2 * STRIPE, STRIPE), STRIPE),
                      pl.ds(pl.multiple_of(x_ % 2 * HEAD, HEAD), HEAD)]

    def q_src(x_):
        return q_hbm.at[pl.ds(pl.multiple_of(x_ // 2 * STRIPE, STRIPE), STRIPE),
                        pl.ds(pl.multiple_of(x_ % 2 * GROUP * HEAD, HEAD), GROUP * HEAD)]

    own_copies = [
        pltpu.make_async_copy(kv_src(k_hbm, x), kv.at[z, x, y, core, 0], loc_sem.at[0]),
        pltpu.make_async_copy(kv_src(v_hbm, x), kv.at[z, x, y, core, 1], loc_sem.at[1]),
        pltpu.make_async_copy(q_src(x), q_in.at[x], loc_sem.at[2]),
        pltpu.make_async_copy(doc_hbm, doc_in.at[x], loc_sem.at[3]),
    ]
    for cp in own_copies:
        cp.start()
    pl.semaphore_wait(barrier, len(peers))

    for y_, d_ in ((y, 0), (1 - y, 1)):
        for x_ in (xs if d_ == 0 else xs + [x]):
            for n, ref in enumerate((k_hbm, v_hbm)):
                send(kv_src(ref, x_), kv.at[z, x, y, core, n], kx_s.at[d_, x_, n], kx_r.at[d_, x, n],
                     dev(z, x_, y_, core, h))
    for x_ in xs:
        to = dev(z, x_, y, core, h)
        send(q_src(x_), q_in.at[x], qx_s.at[x_], qx_r.at[x], to)
        send(doc_hbm, doc_in.at[x], dx_s.at[x_], dx_r.at[x], to)

    def w_rows(x_, k_, i_):
        return pl.ds(pl.multiple_of((x_ * NC + k_) * NPIECE * WROWS + i_ * WROWS, WROWS), WROWS)

    def w_piece(x_, k_, i_):
        return w_far.at[w_rows(x_, k_, i_)]

    for i in range(NPIECE):
        send(w_hbm.at[w_rows(x, core, i), pl.ds(pl.multiple_of((1 - h) * COLS, COLS), COLS)],
             w_piece(x, core, i), wo_s.at[i], wo_r.at[i], outer)

    def w_first(i):
        ref = w_piece(x, core, i)
        got(ref, wo_s.at[i], wo_r.at[i])
        send(ref, ref, wx_s.at[0, i], wx_r.at[0, i], dev(z, right, y, core, h))
        send(ref, ref, wx_s.at[1, i], wx_r.at[1, i], dev(z, left, y, core, h))
        send(ref, ref, wt_s.at[0, i], wt_r.at[0, i], twin)

    def w_second(i):
        for side, (src, dst) in enumerate(((left, right), (right, left))):
            ref = w_piece(src, core, i)
            got(ref, wx_s.at[side, i], wx_r.at[side, i])

            @pl.when(i // (NPIECE // 2) == side)
            def _():
                n = i % (NPIECE // 2)
                send(ref, ref, wy_s.at[side, n], wy_r.at[side, n], dev(z, dst, y, core, h))

            send(ref, ref, wt_s.at[1 + side, i], wt_r.at[1 + side, i], twin)

    def w_third(n):
        for side in range(2):
            i = side * (NPIECE // 2) + n
            ref = w_piece((x + 2) % NX, core, i)
            got(ref, wy_s.at[side, n], wy_r.at[side, n])
            send(ref, ref, wt_s.at[3, i], wt_r.at[3, i], twin)

    w_copy = pltpu.make_async_copy(w_hbm.at[:, pl.ds(pl.multiple_of(h * COLS, COLS), COLS)], w_own, w_sem.at[0])

    def part_ref(zp, part, half=None):
        xb = 2 * (((part + 1) // 2 + 1) % 2)
        yy = (y + part // 2) % 2
        if half is None:
            return kv.at[zp, pl.ds(xb, 2), yy, core]
        return kv.at[zp, pl.ds(xb + half, 1), yy, core]

    def own_part_in(part):
        d_ = part // 2
        for half in range(2):
            x_ = 2 * (((part + 1) // 2 + 1) % 2) + half

            def arrive():
                for n in range(2):
                    got(kv.at[z, x_, (y + d_) % 2, core, n], kx_s.at[d_, x_, n], kx_r.at[d_, x_, n])

            if d_:
                arrive()
            else:
                pl.when(x_ != x)(arrive)

    own_copies[0].wait()
    own_copies[1].wait()
    for part in (0, 1, 2, 3):
        own_part_in(part)
        ref = part_ref(z, part)
        if part < 3:
            send(ref, ref, z_s.at[0, 0, part], z_r.at[0, 0, part], up)
            send(ref, ref, z_s.at[1, 0, part], z_r.at[1, 0, part], down)
        send(ref, ref, c0_s.at[part], c0_r.at[part], twin)
    w_copy.start()

    def twin_ref(zp, part, half=None):
        xb = 2 * (((part + 1) // 2 + 1) % 2)
        yy = (y + part // 2) % 2
        if half is None:
            return kv.at[zp, pl.ds(xb, 2), yy, 1 - core]
        return kv.at[zp, pl.ds(xb + half, 1), yy, 1 - core]

    def work(plane, base, tiles, own, docs):
        def scores(r, b):
            keys = kv[plane, b, :, :, 0].reshape(BLOCK, HEAD)
            s = lax.dot_general(q_rows[base + r], keys, (((1,), (1,)), ((), ())), preferred_element_type=F32)
            if docs:
                kpos = rnd * ROUND + plane * PLANE + b * BLOCK + lax.broadcasted_iota(jnp.int32, (ROWS, BLOCK), 1)
                seen = kpos >= jnp.tile(doc_rows[base + r], (1, BLOCK // HEAD))
                if own:
                    first = rnd * ROUND + (z * 16 + (base + r) * 4 + y * 2 + core) * STRIPE
                    qpos = first + lax.broadcasted_iota(jnp.int32, (ROWS, BLOCK), 0) % STRIPE
                    seen = seen & (kpos <= qpos)
                s = jnp.where(seen, s, MASKED)
            return s

        s = scores(*tiles[0])
        for n, (r, b) in enumerate(tiles):
            ahead = scores(*tiles[n + 1]) if n + 1 < len(tiles) else None
            if b == 0 and own:
                old, total = jnp.full((ROWS, HEAD), MASKED, F32), jnp.zeros((ROWS, 2 * HEAD), F32)
            elif b == 0:
                old, total = top[base + r], acc[base + r]
            new = jnp.maximum(old, jnp.max(s, axis=1, keepdims=True))
            p = jnp.exp2(s * LOG2 - jnp.tile(new * LOG2, (1, BLOCK // HEAD))).astype(BF16)
            shrink = jnp.exp2((old - new) * LOG2)
            values = kv[plane, b, :, :, 1].reshape(BLOCK, HEAD)
            both = jnp.concatenate([values, jnp.ones((BLOCK, HEAD), BF16)], axis=1)
            total = total * jnp.tile(shrink, (1, 2)) + jnp.dot(p, both, preferred_element_type=F32)
            old, s = new, ahead
            if n + 1 == len(tiles) or tiles[n + 1][0] != r:
                acc[base + r] = total
                top[base + r] = old

    every = [(r, b) for r in range(PAIR) for b in range(NX)]

    def chunk(d, side, pair):
        plane = (z + NZ - d + 2 * d * side) % NZ
        earlier = (d > 0) & (plane < z)
        for n in range(NX // PAIR):
            @pl.when((d == 0) & (side == 0) & (pair == n))
            def _():
                work(z, n * PAIR, [(r, b) for r, b in every if b <= n * PAIR + r], True, True)

        @pl.when(earlier & (rnd == 1))
        def _():
            work(plane, pair * PAIR, every, False, True)

        @pl.when(earlier & (rnd == 0))
        def _():
            work(plane, pair * PAIR, every, False, False)

    def event(t, carry):
        s = t // 8 + 1
        e = t % 8
        side, part = e % 2, e // 2
        plane = (z + NZ - s + 2 * s * side) % NZ
        nxt = dev((z + 1 + (NZ - 2) * side) % NZ, x, y, core, h)

        @pl.when((s <= 3) & (part <= 2))
        def _():
            got(part_ref(plane, part), z_s.at[side, s - 1, part], z_r.at[side, s - 1, part])

        @pl.when((s == 4) & (part <= 2))
        def _():
            got(part_ref(plane, part, side), z_s.at[side, 3, part], z_r.at[side, 3, part])

        @pl.when((s <= 3) & (part == 3))
        def _():
            got(part_ref(plane, 3), y_s.at[s - 1, side], y_r.at[s - 1, side])

        @pl.when((s == 4) & (part == 3))
        def _():
            got(part_ref(plane, 3, side), y_s.at[3, side], y_r.at[3, side])

        @pl.when((s <= 2) & (part <= 2))
        def _():
            r = part_ref(plane, part)
            send(r, r, z_s.at[side, s, part], z_r.at[side, s, part], nxt)

        @pl.when((s == 3) & (part <= 2))
        def _():
            r = part_ref(plane, part, side)
            send(r, r, z_s.at[side, 3, part], z_r.at[side, 3, part], nxt)

        @pl.when(s <= 3)
        def _():
            r = part_ref(plane, part)

            @pl.when(part == 0)
            def _():
                send(r, r, y_s.at[s - 1, side], y_r.at[s - 1, side], across)

            send(r, r, c_s.at[s - 1, side, part], c_r.at[s - 1, side, part], twin)

        @pl.when(s == 4)
        def _():
            r = part_ref(plane, part, side)

            @pl.when(part == 0)
            def _():
                send(r, r, y_s.at[3, side], y_r.at[3, side], across)

            send(r, r, c_s.at[3, side, part], c_r.at[3, side, part], twin)

        @pl.when(t == 1)
        def _():
            own_copies[2].wait()
            own_copies[3].wait()
            for x_ in xs:
                got(q_in.at[x_], qx_s.at[x_], qx_r.at[x_])
                got(doc_in.at[x_], dx_s.at[x_], dx_r.at[x_])
            for part_ in range(4):
                got(twin_ref(z, part_), c0_s.at[part_], c0_r.at[part_])
            for rb_ in range(NX):
                line = jnp.broadcast_to(doc_in[rb_].astype(F32), (HEAD, HEAD))
                line = jnp.transpose(line).astype(jnp.int32)
                line = jnp.where(rnd == 1, line[STRIPE:], line[:STRIPE])
                for g in range(GROUP):
                    q_rows[rb_, g * STRIPE:(g + 1) * STRIPE] = q_in[rb_, :, g * HEAD:(g + 1) * HEAD]
                    doc_rows[rb_, g * STRIPE:(g + 1) * STRIPE] = line

        @pl.when(e % 2 == 1)
        def _():
            cs, pair = e // 4, (e // 2) % 2

            @pl.when((s > 1) & (pair == 0))
            def _():
                back = (z + NZ - (s - 1) + 2 * (s - 1) * cs) % NZ
                for part_ in range(4):
                    got(twin_ref(back, part_), c_s.at[s - 2, cs, part_], c_r.at[s - 2, cs, part_])

            chunk(s - 1, cs, pair)

        @pl.when((t % 2 == 1) & (t < 2 * NPIECE))
        def _():
            w_first(t // 2)

        @pl.when((t % 2 == 1) & (t >= WLAG) & (t < WLAG + 2 * NPIECE))
        def _():
            w_second((t - WLAG) // 2)

        return carry

    lax.fori_loop(0, 32, event, 0)

    far = (z + 4) % NZ
    for side in range(2):
        for part in range(4):
            got(twin_ref(far, part, side), c_s.at[3, side, part], c_r.at[3, side, part])

    def place(ref, x_):
        return ref.at[pl.ds(pl.multiple_of(x_ // 2 * STRIPE, STRIPE), STRIPE),
                      pl.ds(pl.multiple_of(x_ % 2 * GROUP * HEAD, HEAD), GROUP * HEAD)]

    def last(pair, carry):
        chunk(4, 0, pair)

        def finish(r, inner):
            rb = pair * PAIR + r
            total = acc[rb]
            o = (total[:, :HEAD] / total[:, HEAD:]).astype(BF16)
            for g in range(GROUP):
                attn_send[rb, :, g * HEAD:(g + 1) * HEAD] = o[g * STRIPE:(g + 1) * STRIPE]
            send(attn_send.at[rb], place(attn_far, x), of_s.at[rb], of_r.at[x], dev(z, rb, y, core, 1 - h))

            @pl.when(rb != x)
            def _():
                send(attn_send.at[rb], place(attn_in, x), o_s.at[rb], o_r.at[x], dev(z, rb, y, core, h))

            return inner

        return lax.fori_loop(0, PAIR, finish, carry)

    lax.fori_loop(0, NX // PAIR, last, 0)
    home = pltpu.make_async_copy(attn_send.at[x], place(attn_in, x), loc_sem.at[0])
    home.start()
    for part in range(4):
        sent(part_ref(z, part), c0_s.at[part], c0_r.at[part])
    for n in range(4):
        for side in range(2):
            half = side if n == 3 else None
            for part in range(3):
                sent(part_ref(z, part, half), z_s.at[side, n, part], z_r.at[side, n, part])
            for part in range(4):
                sent(part_ref(z, part, half), c_s.at[n, side, part], c_r.at[n, side, part])
            sent(part_ref(z, 0, half), y_s.at[n, side], y_r.at[n, side])

    for n in range(NPIECE // 2):
        w_third(n)

    def near(j, carry):
        cols = pl.ds(pl.multiple_of(j * CHUNK, CHUNK), CHUNK)
        own_part[:, cols] = jnp.dot(attn_in[...], w_own[:, cols], preferred_element_type=F32)
        return carry

    def far_too(j, carry):
        cols = pl.ds(pl.multiple_of(j * CHUNK, CHUNK), CHUNK)
        rest = jnp.dot(attn_far[...], w_far[:, cols], preferred_element_type=F32)
        out_ref[:, cols] = (own_part[:, cols] + rest).astype(BF16)
        return carry

    w_copy.wait()
    home.wait()
    for x_ in xs:
        got(place(attn_in, x_), o_s.at[x_], o_r.at[x_])
    lax.fori_loop(0, NCH, near, 0)
    for x_ in xs:
        for n in range(2):
            for d_ in range(2):
                sent(kv.at[z, x_, y, core, n], kx_s.at[d_, x_, n], kx_r.at[d_, x_, n])
        sent(q_in.at[x_], qx_s.at[x_], qx_r.at[x_])
        sent(doc_in.at[x_], dx_s.at[x_], dx_r.at[x_])
        sent(attn_send.at[x_], o_s.at[x_], o_r.at[x_])
    for x_ in range(NX):
        sent(attn_send.at[x_], of_s.at[x_], of_r.at[x_])
    for i in range(NPIECE):
        ref = w_piece(x, core, i)
        sent(ref, wo_s.at[i], wo_r.at[i])
        for side in range(2):
            sent(ref, wx_s.at[side, i], wx_r.at[side, i])
        for hop in range(4):
            sent(ref, wt_s.at[hop, i], wt_r.at[hop, i])
    for n in range(NPIECE // 2):
        for side in range(2):
            sent(w_piece(x, core, n), wy_s.at[side, n], wy_r.at[side, n])
    for n in range(2):
        sent(kv.at[z, x, y, core, n], kx_s.at[1, x, n], kx_r.at[1, x, n])

    for hop, x_ in enumerate((x, left, right, (x + 2) % NX)):
        for i in range(NPIECE):
            got(w_piece(x_, 1 - core, i), wt_s.at[hop, i], wt_r.at[hop, i])
    for x_ in range(NX):
        got(place(attn_far, x_), of_s.at[x_], of_r.at[x_])
    lax.fori_loop(0, NCH, far_too, 0)


def local(queries, keys, values, doc_start, out_weight):
    docs = doc_start.reshape(1, doc_start.shape[0])
    dma = pltpu.SemaphoreType.DMA
    anyspace = pl.BlockSpec(memory_space=pl.ANY)
    return pl.pallas_call(
        kernel,
        out_shape=jax.ShapeDtypeStruct((2 * STRIPE, COLS), BF16),
        in_specs=[anyspace] * 5,
        out_specs=pl.BlockSpec(memory_space=pltpu.VMEM),
        scratch_shapes=[
            pltpu.VMEM((NZ, NX, NY, NC, 2, STRIPE, HEAD), BF16),
            pltpu.VMEM((NX, STRIPE, GROUP * HEAD), BF16),
            pltpu.VMEM((NX, 1, HEAD), jnp.int32),
            pltpu.VMEM((NX, ROWS, HEAD), BF16),
            pltpu.VMEM((NX, ROWS, HEAD), jnp.int32),
            pltpu.VMEM((NX, ROWS, HEAD), F32),
            pltpu.VMEM((NX, ROWS, 2 * HEAD), F32),
            pltpu.VMEM((NX, STRIPE, GROUP * HEAD), BF16),
            pltpu.VMEM((2 * STRIPE, 2 * GROUP * HEAD), BF16),
            pltpu.VMEM((2 * STRIPE, 2 * GROUP * HEAD), BF16),
            pltpu.VMEM((2 * GROUP * HEAD, COLS), BF16),
            pltpu.VMEM((2 * GROUP * HEAD, COLS), BF16),
            pltpu.VMEM((2 * STRIPE, COLS), F32),
            dma((4,)), dma((1,)),
            dma((2, NX, 2)), dma((2, NX, 2)), dma((NX,)), dma((NX,)), dma((NX,)), dma((NX,)),
            dma((2, 4, 3)), dma((2, 4, 3)), dma((4,)), dma((4,)), dma((4, 2, 4)), dma((4, 2, 4)),
            dma((4, 2)), dma((4, 2)), dma((NX,)), dma((NX,)),
            dma((NX,)), dma((NX,)), dma((NPIECE,)), dma((NPIECE,)), dma((2, NPIECE)), dma((2, NPIECE)),
            dma((2, NPIECE // 2)), dma((2, NPIECE // 2)), dma((4, NPIECE)), dma((4, NPIECE)),
        ],
        compiler_params=pltpu.CompilerParams(
            collective_id=0, has_side_effects=True, vmem_limit_bytes=56 * 1024 * 1024),
    )(queries, keys, values, docs, out_weight)


def solution(mesh):
    placed = (P("ctx", "head"), P("ctx", "head"), P("ctx", "head"), P("ctx"), P("head", None))
    return jax.shard_map(local, mesh=mesh, in_specs=placed, out_specs=P("ctx", "head"), check_vma=False)
```

```python
import math

import jax
import jax.numpy as jnp
from jax import lax
from jax.experimental import pallas as pl
from jax.experimental.pallas import tpu as pltpu
from jax.sharding import PartitionSpec as P

NZ, NX, NY, NC = 8, 4, 2, 2
STRIPE = 64
HEAD = 128
GROUP = 4
PLANE = NX * NY * NC * STRIPE
ROWS = GROUP * STRIPE
BLOCK = NY * NC * STRIPE
ROUND = NZ * PLANE
COLS = 2048
CHUNK = 2048
NCH = COLS // CHUNK
NPIECE = 4
WROWS = 2 * GROUP * HEAD // (NX * NC * NPIECE)
WLAG = 18
PAIR = 2
MASKED = -1e30
LOG2 = math.log2(math.e) / math.sqrt(HEAD)
MESH = pl.DeviceIdType.MESH
F32 = jnp.float32
BF16 = jnp.bfloat16


def kernel(q_hbm, k_hbm, v_hbm, doc_hbm, w_hbm, out_ref,
           kv, q_in, doc_in, q_rows, doc_rows, top, acc, attn_send, attn_in, attn_far, w_own, w_far,
           own_part,
           loc_sem, w_sem, kx_s, kx_r, qx_s, qx_r, dx_s, dx_r, z_s, z_r, c0_s, c0_r, c_s, c_r,
           y_s, y_r, o_s, o_r, of_s, of_r, wo_s, wo_r, wx_s, wx_r, wy_s, wy_r, wt_s, wt_r):
    c = lax.axis_index("ctx")
    h = lax.axis_index("head")
    z, x, y, core = c // 16, (c // 4) % NX, (c // 2) % NY, c % NC
    rnd = x // 2

    def dev(z_, x_, y_, k_, h_):
        return (((z_ * NX + x_) * NY + y_) * NC + k_, h_)

    up = dev((z + 1) % NZ, x, y, core, h)
    down = dev((z + NZ - 1) % NZ, x, y, core, h)
    across = dev(z, x, 1 - y, core, h)
    twin = dev(z, x, y, 1 - core, h)
    outer = dev(z, x, 1 - y, core, 1 - h)
    right, left = (x + 1) % NX, (x + NX - 1) % NX
    xs = [(x + d) % NX for d in (2, 1, 3)]

    def send(src, dst, ss, rs, to):
        cp = pltpu.make_async_remote_copy(src, dst, ss, rs, device_id=to, device_id_type=MESH)
        cp.start()

    def got(ref, ss, rs):
        pltpu.make_async_remote_copy(ref, ref, ss, rs, device_id=twin, device_id_type=MESH).wait_recv()

    def sent(ref, ss, rs):
        pltpu.make_async_remote_copy(ref, ref, ss, rs, device_id=twin, device_id_type=MESH).wait_send()

    barrier = pltpu.get_barrier_semaphore()
    peers = [up, down, across, twin, outer] + [dev(z, x_, y, core, h) for x_ in xs]
    peers += [dev(z, x_, 1 - y, core, h) for x_ in xs]
    peers += [dev(z, x_, y, core, 1 - h) for x_ in range(NX)]
    for peer in peers:
        pl.semaphore_signal(barrier, inc=1, device_id=peer, device_id_type=MESH)

    def kv_src(ref, x_):
        return ref.at[pl.ds(pl.multiple_of(x_ // 2 * STRIPE, STRIPE), STRIPE),
                      pl.ds(pl.multiple_of(x_ % 2 * HEAD, HEAD), HEAD)]

    def q_src(x_):
        return q_hbm.at[pl.ds(pl.multiple_of(x_ // 2 * STRIPE, STRIPE), STRIPE),
                        pl.ds(pl.multiple_of(x_ % 2 * GROUP * HEAD, HEAD), GROUP * HEAD)]

    own_copies = [
        pltpu.make_async_copy(kv_src(k_hbm, x), kv.at[z, x, y, core, 0], loc_sem.at[0]),
        pltpu.make_async_copy(kv_src(v_hbm, x), kv.at[z, x, y, core, 1], loc_sem.at[1]),
        pltpu.make_async_copy(q_src(x), q_in.at[x], loc_sem.at[2]),
        pltpu.make_async_copy(doc_hbm, doc_in.at[x], loc_sem.at[3]),
    ]
    for cp in own_copies:
        cp.start()
    pl.semaphore_wait(barrier, len(peers))

    for y_, d_ in ((y, 0), (1 - y, 1)):
        for x_ in (xs if d_ == 0 else xs + [x]):
            for n, ref in enumerate((k_hbm, v_hbm)):
                send(kv_src(ref, x_), kv.at[z, x, y, core, n], kx_s.at[d_, x_, n], kx_r.at[d_, x, n],
                     dev(z, x_, y_, core, h))
    for x_ in xs:
        to = dev(z, x_, y, core, h)
        send(q_src(x_), q_in.at[x], qx_s.at[x_], qx_r.at[x], to)
        send(doc_hbm, doc_in.at[x], dx_s.at[x_], dx_r.at[x], to)

    def w_rows(x_, k_, i_):
        return pl.ds(pl.multiple_of((x_ * NC + k_) * NPIECE * WROWS + i_ * WROWS, WROWS), WROWS)

    def w_piece(x_, k_, i_):
        return w_far.at[w_rows(x_, k_, i_)]

    for i in range(NPIECE):
        send(w_hbm.at[w_rows(x, core, i), pl.ds(pl.multiple_of((1 - h) * COLS, COLS), COLS)],
             w_piece(x, core, i), wo_s.at[i], wo_r.at[i], outer)

    def w_first(i):
        ref = w_piece(x, core, i)
        got(ref, wo_s.at[i], wo_r.at[i])
        send(ref, ref, wx_s.at[0, i], wx_r.at[0, i], dev(z, right, y, core, h))
        send(ref, ref, wx_s.at[1, i], wx_r.at[1, i], dev(z, left, y, core, h))
        send(ref, ref, wt_s.at[0, i], wt_r.at[0, i], twin)

    def w_second(i):
        for side, (src, dst) in enumerate(((left, right), (right, left))):
            ref = w_piece(src, core, i)
            got(ref, wx_s.at[side, i], wx_r.at[side, i])

            @pl.when(i // (NPIECE // 2) == side)
            def _():
                n = i % (NPIECE // 2)
                send(ref, ref, wy_s.at[side, n], wy_r.at[side, n], dev(z, dst, y, core, h))

            send(ref, ref, wt_s.at[1 + side, i], wt_r.at[1 + side, i], twin)

    def w_third(n):
        for side in range(2):
            i = side * (NPIECE // 2) + n
            ref = w_piece((x + 2) % NX, core, i)
            got(ref, wy_s.at[side, n], wy_r.at[side, n])
            send(ref, ref, wt_s.at[3, i], wt_r.at[3, i], twin)

    w_copy = pltpu.make_async_copy(w_hbm.at[:, pl.ds(pl.multiple_of(h * COLS, COLS), COLS)], w_own, w_sem.at[0])

    def part_ref(zp, part, half=None):
        xb = 2 * (((part + 1) // 2 + 1) % 2)
        yy = (y + part // 2) % 2
        if half is None:
            return kv.at[zp, pl.ds(xb, 2), yy, core]
        return kv.at[zp, pl.ds(xb + half, 1), yy, core]

    def own_part_in(part):
        d_ = part // 2
        for half in range(2):
            x_ = 2 * (((part + 1) // 2 + 1) % 2) + half

            def arrive():
                for n in range(2):
                    got(kv.at[z, x_, (y + d_) % 2, core, n], kx_s.at[d_, x_, n], kx_r.at[d_, x_, n])

            if d_:
                arrive()
            else:
                pl.when(x_ != x)(arrive)

    own_copies[0].wait()
    own_copies[1].wait()
    for part in (0, 1, 2, 3):
        own_part_in(part)
        ref = part_ref(z, part)
        if part < 3:
            send(ref, ref, z_s.at[0, 0, part], z_r.at[0, 0, part], up)
            send(ref, ref, z_s.at[1, 0, part], z_r.at[1, 0, part], down)
        send(ref, ref, c0_s.at[part], c0_r.at[part], twin)
    w_copy.start()

    def twin_ref(zp, part, half=None):
        xb = 2 * (((part + 1) // 2 + 1) % 2)
        yy = (y + part // 2) % 2
        if half is None:
            return kv.at[zp, pl.ds(xb, 2), yy, 1 - core]
        return kv.at[zp, pl.ds(xb + half, 1), yy, 1 - core]

    def work(plane, base, tiles, own, docs):
        def scores(r, b):
            keys = kv[plane, b, :, :, 0].reshape(BLOCK, HEAD)
            s = lax.dot_general(q_rows[base + r], keys, (((1,), (1,)), ((), ())), preferred_element_type=F32)
            if docs:
                kpos = rnd * ROUND + plane * PLANE + b * BLOCK + lax.broadcasted_iota(jnp.int32, (ROWS, BLOCK), 1)
                seen = kpos >= jnp.tile(doc_rows[base + r], (1, BLOCK // HEAD))
                if own:
                    first = rnd * ROUND + (z * 16 + (base + r) * 4 + y * 2 + core) * STRIPE
                    qpos = first + lax.broadcasted_iota(jnp.int32, (ROWS, BLOCK), 0) % STRIPE
                    seen = seen & (kpos <= qpos)
                s = jnp.where(seen, s, MASKED)
            return s

        s = scores(*tiles[0])
        for n, (r, b) in enumerate(tiles):
            ahead = scores(*tiles[n + 1]) if n + 1 < len(tiles) else None
            if b == 0 and own:
                old, total = jnp.full((ROWS, HEAD), MASKED, F32), jnp.zeros((ROWS, 2 * HEAD), F32)
            elif b == 0:
                old, total = top[base + r], acc[base + r]
            new = jnp.maximum(old, jnp.max(s, axis=1, keepdims=True))
            p = jnp.exp2(s * LOG2 - jnp.tile(new * LOG2, (1, BLOCK // HEAD))).astype(BF16)
            shrink = jnp.exp2((old - new) * LOG2)
            values = kv[plane, b, :, :, 1].reshape(BLOCK, HEAD)
            both = jnp.concatenate([values, jnp.ones((BLOCK, HEAD), BF16)], axis=1)
            total = total * jnp.tile(shrink, (1, 2)) + jnp.dot(p, both, preferred_element_type=F32)
            old, s = new, ahead
            if n + 1 == len(tiles) or tiles[n + 1][0] != r:
                acc[base + r] = total
                top[base + r] = old

    every = [(r, b) for r in range(PAIR) for b in range(NX)]

    def chunk(d, side, pair):
        plane = (z + NZ - d + 2 * d * side) % NZ
        earlier = (d > 0) & (plane < z)
        for n in range(NX // PAIR):
            @pl.when((d == 0) & (side == 0) & (pair == n))
            def _():
                work(z, n * PAIR, [(r, b) for r, b in every if b <= n * PAIR + r], True, True)

        @pl.when(earlier & (rnd == 1))
        def _():
            work(plane, pair * PAIR, every, False, True)

        @pl.when(earlier & (rnd == 0))
        def _():
            work(plane, pair * PAIR, every, False, False)

    def event(t, carry):
        s = t // 8 + 1
        e = t % 8
        side, part = e % 2, e // 2
        plane = (z + NZ - s + 2 * s * side) % NZ
        nxt = dev((z + 1 + (NZ - 2) * side) % NZ, x, y, core, h)

        @pl.when((s <= 3) & (part <= 2))
        def _():
            got(part_ref(plane, part), z_s.at[side, s - 1, part], z_r.at[side, s - 1, part])

        @pl.when((s == 4) & (part <= 2))
        def _():
            got(part_ref(plane, part, side), z_s.at[side, 3, part], z_r.at[side, 3, part])

        @pl.when((s <= 3) & (part == 3))
        def _():
            got(part_ref(plane, 3), y_s.at[s - 1, side], y_r.at[s - 1, side])

        @pl.when((s == 4) & (part == 3))
        def _():
            got(part_ref(plane, 3, side), y_s.at[3, side], y_r.at[3, side])

        @pl.when((s <= 2) & (part <= 2))
        def _():
            r = part_ref(plane, part)
            send(r, r, z_s.at[side, s, part], z_r.at[side, s, part], nxt)

        @pl.when((s == 3) & (part <= 2))
        def _():
            r = part_ref(plane, part, side)
            send(r, r, z_s.at[side, 3, part], z_r.at[side, 3, part], nxt)

        @pl.when(s <= 3)
        def _():
            r = part_ref(plane, part)

            @pl.when(part == 0)
            def _():
                send(r, r, y_s.at[s - 1, side], y_r.at[s - 1, side], across)

            send(r, r, c_s.at[s - 1, side, part], c_r.at[s - 1, side, part], twin)

        @pl.when(s == 4)
        def _():
            r = part_ref(plane, part, side)

            @pl.when(part == 0)
            def _():
                send(r, r, y_s.at[3, side], y_r.at[3, side], across)

            send(r, r, c_s.at[3, side, part], c_r.at[3, side, part], twin)

        @pl.when(t == 1)
        def _():
            own_copies[2].wait()
            own_copies[3].wait()
            for x_ in xs:
                got(q_in.at[x_], qx_s.at[x_], qx_r.at[x_])
                got(doc_in.at[x_], dx_s.at[x_], dx_r.at[x_])
            for part_ in range(4):
                got(twin_ref(z, part_), c0_s.at[part_], c0_r.at[part_])
            for rb_ in range(NX):
                line = jnp.broadcast_to(doc_in[rb_].astype(F32), (HEAD, HEAD))
                line = jnp.transpose(line).astype(jnp.int32)
                line = jnp.where(rnd == 1, line[STRIPE:], line[:STRIPE])
                for g in range(GROUP):
                    q_rows[rb_, g * STRIPE:(g + 1) * STRIPE] = q_in[rb_, :, g * HEAD:(g + 1) * HEAD]
                    doc_rows[rb_, g * STRIPE:(g + 1) * STRIPE] = line

        @pl.when(e % 2 == 1)
        def _():
            cs, pair = e // 4, (e // 2) % 2

            @pl.when((s > 1) & (pair == 0))
            def _():
                back = (z + NZ - (s - 1) + 2 * (s - 1) * cs) % NZ
                for part_ in range(4):
                    got(twin_ref(back, part_), c_s.at[s - 2, cs, part_], c_r.at[s - 2, cs, part_])

            chunk(s - 1, cs, pair)

        @pl.when((t % 2 == 0) & (t < 2 * NPIECE))
        def _():
            w_first(t // 2)

        @pl.when((t % 2 == 0) & (t >= WLAG) & (t < WLAG + 2 * NPIECE))
        def _():
            w_second((t - WLAG) // 2)

        return carry

    lax.fori_loop(0, 32, event, 0)

    far = (z + 4) % NZ
    for side in range(2):
        for part in range(4):
            got(twin_ref(far, part, side), c_s.at[3, side, part], c_r.at[3, side, part])

    def place(ref, x_):
        return ref.at[pl.ds(pl.multiple_of(x_ // 2 * STRIPE, STRIPE), STRIPE),
                      pl.ds(pl.multiple_of(x_ % 2 * GROUP * HEAD, HEAD), GROUP * HEAD)]

    def last(pair, carry):
        chunk(4, 0, pair)

        def finish(r, inner):
            rb = pair * PAIR + r
            total = acc[rb]
            o = (total[:, :HEAD] / total[:, HEAD:]).astype(BF16)
            for g in range(GROUP):
                attn_send[rb, :, g * HEAD:(g + 1) * HEAD] = o[g * STRIPE:(g + 1) * STRIPE]
            send(attn_send.at[rb], place(attn_far, x), of_s.at[rb], of_r.at[x], dev(z, rb, y, core, 1 - h))

            @pl.when(rb != x)
            def _():
                send(attn_send.at[rb], place(attn_in, x), o_s.at[rb], o_r.at[x], dev(z, rb, y, core, h))

            return inner

        return lax.fori_loop(0, PAIR, finish, carry)

    lax.fori_loop(0, NX // PAIR, last, 0)
    home = pltpu.make_async_copy(attn_send.at[x], place(attn_in, x), loc_sem.at[0])
    home.start()
    for part in range(4):
        sent(part_ref(z, part), c0_s.at[part], c0_r.at[part])
    for n in range(4):
        for side in range(2):
            half = side if n == 3 else None
            for part in range(3):
                sent(part_ref(z, part, half), z_s.at[side, n, part], z_r.at[side, n, part])
            for part in range(4):
                sent(part_ref(z, part, half), c_s.at[n, side, part], c_r.at[n, side, part])
            sent(part_ref(z, 0, half), y_s.at[n, side], y_r.at[n, side])

    for n in range(NPIECE // 2):
        w_third(n)

    def near(j, carry):
        cols = pl.ds(pl.multiple_of(j * CHUNK, CHUNK), CHUNK)
        own_part[:, cols] = jnp.dot(attn_in[...], w_own[:, cols], preferred_element_type=F32)
        return carry

    def far_too(j, carry):
        cols = pl.ds(pl.multiple_of(j * CHUNK, CHUNK), CHUNK)
        rest = jnp.dot(attn_far[...], w_far[:, cols], preferred_element_type=F32)
        out_ref[:, cols] = (own_part[:, cols] + rest).astype(BF16)
        return carry

    w_copy.wait()
    home.wait()
    for x_ in xs:
        got(place(attn_in, x_), o_s.at[x_], o_r.at[x_])
    lax.fori_loop(0, NCH, near, 0)
    for x_ in xs:
        for n in range(2):
            for d_ in range(2):
                sent(kv.at[z, x_, y, core, n], kx_s.at[d_, x_, n], kx_r.at[d_, x_, n])
        sent(q_in.at[x_], qx_s.at[x_], qx_r.at[x_])
        sent(doc_in.at[x_], dx_s.at[x_], dx_r.at[x_])
        sent(attn_send.at[x_], o_s.at[x_], o_r.at[x_])
    for x_ in range(NX):
        sent(attn_send.at[x_], of_s.at[x_], of_r.at[x_])
    for i in range(NPIECE):
        ref = w_piece(x, core, i)
        sent(ref, wo_s.at[i], wo_r.at[i])
        for side in range(2):
            sent(ref, wx_s.at[side, i], wx_r.at[side, i])
        for hop in range(4):
            sent(ref, wt_s.at[hop, i], wt_r.at[hop, i])
    for n in range(NPIECE // 2):
        for side in range(2):
            sent(w_piece(x, core, n), wy_s.at[side, n], wy_r.at[side, n])
    for n in range(2):
        sent(kv.at[z, x, y, core, n], kx_s.at[1, x, n], kx_r.at[1, x, n])

    for hop, x_ in enumerate((x, left, right, (x + 2) % NX)):
        for i in range(NPIECE):
            got(w_piece(x_, 1 - core, i), wt_s.at[hop, i], wt_r.at[hop, i])
    for x_ in range(NX):
        got(place(attn_far, x_), of_s.at[x_], of_r.at[x_])
    lax.fori_loop(0, NCH, far_too, 0)


def local(queries, keys, values, doc_start, out_weight):
    docs = doc_start.reshape(1, doc_start.shape[0])
    dma = pltpu.SemaphoreType.DMA
    anyspace = pl.BlockSpec(memory_space=pl.ANY)
    return pl.pallas_call(
        kernel,
        out_shape=jax.ShapeDtypeStruct((2 * STRIPE, COLS), BF16),
        in_specs=[anyspace] * 5,
        out_specs=pl.BlockSpec(memory_space=pltpu.VMEM),
        scratch_shapes=[
            pltpu.VMEM((NZ, NX, NY, NC, 2, STRIPE, HEAD), BF16),
            pltpu.VMEM((NX, STRIPE, GROUP * HEAD), BF16),
            pltpu.VMEM((NX, 1, HEAD), jnp.int32),
            pltpu.VMEM((NX, ROWS, HEAD), BF16),
            pltpu.VMEM((NX, ROWS, HEAD), jnp.int32),
            pltpu.VMEM((NX, ROWS, HEAD), F32),
            pltpu.VMEM((NX, ROWS, 2 * HEAD), F32),
            pltpu.VMEM((NX, STRIPE, GROUP * HEAD), BF16),
            pltpu.VMEM((2 * STRIPE, 2 * GROUP * HEAD), BF16),
            pltpu.VMEM((2 * STRIPE, 2 * GROUP * HEAD), BF16),
            pltpu.VMEM((2 * GROUP * HEAD, COLS), BF16),
            pltpu.VMEM((2 * GROUP * HEAD, COLS), BF16),
            pltpu.VMEM((2 * STRIPE, COLS), F32),
            dma((4,)), dma((1,)),
            dma((2, NX, 2)), dma((2, NX, 2)), dma((NX,)), dma((NX,)), dma((NX,)), dma((NX,)),
            dma((2, 4, 3)), dma((2, 4, 3)), dma((4,)), dma((4,)), dma((4, 2, 4)), dma((4, 2, 4)),
            dma((4, 2)), dma((4, 2)), dma((NX,)), dma((NX,)),
            dma((NX,)), dma((NX,)), dma((NPIECE,)), dma((NPIECE,)), dma((2, NPIECE)), dma((2, NPIECE)),
            dma((2, NPIECE // 2)), dma((2, NPIECE // 2)), dma((4, NPIECE)), dma((4, NPIECE)),
        ],
        compiler_params=pltpu.CompilerParams(
            collective_id=0, has_side_effects=True, vmem_limit_bytes=56 * 1024 * 1024),
    )(queries, keys, values, docs, out_weight)


def solution(mesh):
    placed = (P("ctx", "head"), P("ctx", "head"), P("ctx", "head"), P("ctx"), P("head", None))
    return jax.shard_map(local, mesh=mesh, in_specs=placed, out_specs=P("ctx", "head"), check_vma=False)
```
